256 devices in a mesh: rows: 32 (over z, x_hi, core), lev: 8 (over y, x_lo).
Axes of the slice: x: 4 (x_hi: 2, x_lo: 2; x = x_hi * 2 + x_lo), y: 4, z: 8, core: 2. Of those that a mesh axis runs over, the one named last changes fastest.
Arguments:
- field: bfloat16 [2, 8, 512, 64, 1024], P(None, 'lev', 'rows'), may hold values from -6 to 6
- spectral_weight: bfloat16 [3, 64, 64, 64, 64], P(None, None, 'rows'), may hold values from -5 to 5
- local_weight: bfloat16 [64, 64], replicated, may hold values from -0.75 to 0.75
- local_bias: float32 [64], replicated, may hold values from -4 to 4
- gate_weight: bfloat16 [64, 256], replicated, may hold values from -0.75 to 0.75
- up_weight: bfloat16 [64, 256], replicated, may hold values from -0.75 to 0.75
- down_weight: bfloat16 [256, 64], replicated, may hold values from -0.375 to 0.375
Outputs:
- updated: bfloat16 [2, 8, 512, 64, 1024], P(None, 'lev', 'rows')
The draws below stay inside these ranges and needn't reach their ends.
All inputs are finite; a program needn't handle non-finite values.
Results may differ from the reference program's by a relative error of at most 0.02.
Values may be sent and summed in bfloat16 or wider, within the bound.
A program may use at most 128 MiB of HBM per device.

```python
import math
import jax
import jax.numpy as jnp
from jax import lax

B = 2
LEV = 8
NLON = 1024
C = 64
HID = 256
KLAT = 64
KLON = 64
NLAT = 512


def shard_levels(stream_key, dims, split, least, largest):
    def one(axis_at, parts):
        heights = jax.random.uniform(jax.random.fold_in(jax.random.fold_in(stream_key, 6), axis_at), (parts,), jnp.float32, least / len(split), largest / len(split))
        return jnp.repeat(jnp.exp(heights), dims[axis_at] // parts).reshape((-1,) + (1,) * (len(dims) - axis_at - 1))

    loudness = one(*split[0])
    for cut in split[1:]:
        loudness = loudness * one(*cut)
    return loudness


def centred(key, dims, width, bound, split=(), kind=jnp.bfloat16):
    gain = shard_levels(key, dims, split, -0.22, 0.18) if split else 1.0
    array = jax.random.normal(key, dims, jnp.float32) * width * gain
    return jnp.minimum(jnp.maximum(array, -bound), bound).astype(kind)


def setup_inputs(seed: int = 0) -> dict:
    arg_keys = jax.random.split(jax.random.key(seed), 8)
    field = centred(arg_keys[0], (B, LEV, NLAT, C, NLON), 1.0, 6.0, ((1, 8), (2, 32)))
    spectral_weight = centred(arg_keys[1], (3, KLAT, KLON, C, C), 0.8, 5.0, ((2, 32),))
    local_weight = centred(arg_keys[2], (C, C), C ** -0.5, 0.75)
    local_bias = centred(arg_keys[3], (C,), 1.0, 4.0, (), jnp.float32)
    gate_weight = centred(arg_keys[4], (C, HID), C ** -0.5, 0.75)
    up_weight = centred(arg_keys[5], (C, HID), C ** -0.5, 0.75)
    down_weight = centred(arg_keys[6], (HID, C), HID ** -0.5, 0.375)
    return dict(field=field, spectral_weight=spectral_weight, local_weight=local_weight, local_bias=local_bias, gate_weight=gate_weight, up_weight=up_weight, down_weight=down_weight)


def cas_rows(positions, count, modes):
    freq = jnp.arange(modes, dtype=jnp.int32) - modes // 2
    turns = positions[:, None] * freq[None, :] % count
    angle = 2.0 * math.pi / count * turns.astype(jnp.float32)
    return (jnp.cos(angle) + jnp.sin(angle)) / math.sqrt(count)

def rounded(value):
    return lax.optimization_barrier(value.astype(jnp.bfloat16))

def reference(field, spectral_weight, local_weight, local_bias, gate_weight, up_weight, down_weight):
    high = lax.Precision.HIGHEST
    lon_table = cas_rows(jnp.arange(NLON, dtype=jnp.int32), NLON, KLON).astype(jnp.bfloat16)
    lat_table = cas_rows(jnp.arange(NLAT, dtype=jnp.int32), NLAT, KLAT)
    along = jnp.dot(field.reshape(-1, NLON), lon_table, preferred_element_type=jnp.float32)
    along = along.reshape(B, LEV, NLAT, C, KLON)
    modes = jnp.einsum('nk,blncm->blkcm', lat_table, along, precision=high)
    modes_b = rounded(modes).astype(jnp.float32)
    padded = jnp.pad(modes_b, ((0, 0), (1, 1), (0, 0), (0, 0), (0, 0)))
    mixed = jnp.zeros((B, LEV, KLAT, C, KLON), jnp.float32)
    for shift_level in range(3):
        mixed = mixed + jnp.einsum('kmco,blkcm->blkom', spectral_weight[shift_level].astype(jnp.float32), padded[:, shift_level:shift_level + LEV], precision=high)
    mixed_b = rounded(mixed).astype(jnp.float32)
    back = jnp.einsum('nk,blkom->blnom', lat_table, mixed_b, precision=high)
    back_b = rounded(back)
    local_f = local_weight.astype(jnp.float32)
    gate_f = gate_weight.astype(jnp.float32)
    up_f = up_weight.astype(jnp.float32)
    down_f = down_weight.astype(jnp.float32)

    def finish(pair):
        grid, coarse = pair
        spectral = jnp.dot(coarse.reshape(-1, KLON), lon_table.T, preferred_element_type=jnp.float32)
        spectral = spectral.reshape(NLAT, C, NLON)
        grid_f = grid.astype(jnp.float32)
        local = jnp.einsum('co,ncx->nox', local_f, grid_f, precision=high)
        value = spectral + local + local_bias[None, :, None]
        act = rounded(jax.nn.gelu(value, approximate=False)).astype(jnp.float32)
        gate = jnp.einsum('ch,ncx->nhx', gate_f, act, precision=high)
        upper = jnp.einsum('ch,ncx->nhx', up_f, act, precision=high)
        hidden = rounded(jax.nn.silu(gate) * upper).astype(jnp.float32)
        down = jnp.einsum('hc,nhx->ncx', down_f, hidden, precision=high)
        return (grid_f + down).astype(jnp.bfloat16)
    result = lax.map(finish, (field.reshape(B * LEV, NLAT, C, NLON), back_b.reshape(B * LEV, NLAT, C, KLON)))
    return result.reshape(B, LEV, NLAT, C, NLON)
```

```python
import math

import jax
import jax.numpy as jnp
from jax import lax
from jax.sharding import PartitionSpec as P


def extended(cells, sides, width):
    for axis, dim in sides:
        count = lax.axis_size(axis)
        ends = count - 1
        head = lax.slice_in_dim(cells, 0, width, axis=dim)
        tail = lax.slice_in_dim(cells, cells.shape[dim] - width, cells.shape[dim], axis=dim)
        cells = jnp.concatenate(
            [
                lax.ppermute(tail, axis, [(i, (i + 1) % count) for i in range(ends)]),
                cells,
                lax.ppermute(head, axis, [((i + 1) % count, i) for i in range(ends)]),
            ],
            axis=dim,
        )
    return cells


def cas_rows(positions, count, modes):
    freq = jnp.arange(modes, dtype=jnp.int32) - modes // 2
    turns = positions[:, None] * freq[None, :] % count
    angle = 2.0 * math.pi / count * turns.astype(jnp.float32)
    return (jnp.cos(angle) + jnp.sin(angle)) / math.sqrt(count)


def body(field, spectral_weight, local_weight, local_bias, gate_weight, up_weight, down_weight):
    high = lax.Precision.HIGHEST
    batch, levels, lat_rows, chans, lon_cells = field.shape
    ranks = lax.axis_size("rows")
    lat_total = lat_rows * ranks
    lat_modes = spectral_weight.shape[1]
    lon_modes = spectral_weight.shape[2] * ranks
    lon_table = cas_rows(jnp.arange(lon_cells, dtype=jnp.int32), lon_cells, lon_modes).astype(
        jnp.bfloat16
    )
    own_rows = lax.axis_index("rows") * lat_rows + jnp.arange(lat_rows, dtype=jnp.int32)
    own_table = cas_rows(own_rows, lat_total, lat_modes)
    along = jnp.einsum("xm,blncx->mblnc", lon_table, field, preferred_element_type=jnp.float32)
    partial_modes = jnp.einsum("nk,mblnc->mblkc", own_table, along, precision=high)
    modes = lax.psum_scatter(
        partial_modes.astype(jnp.bfloat16), "rows", scatter_dimension=0, tiled=True
    )
    padded = extended(modes, (("lev", 2),), 1)
    mixed = jnp.einsum(
        "kjco,jblkc->jblko",
        spectral_weight[0],
        padded[:, :, 0:levels],
        preferred_element_type=jnp.float32,
    )
    mixed = mixed + jnp.einsum(
        "kjco,jblkc->jblko",
        spectral_weight[1],
        padded[:, :, 1 : levels + 1],
        preferred_element_type=jnp.float32,
    )
    mixed = mixed + jnp.einsum(
        "kjco,jblkc->jblko",
        spectral_weight[2],
        padded[:, :, 2 : levels + 2],
        preferred_element_type=jnp.float32,
    )
    mixed_b = mixed.astype(jnp.bfloat16)
    gathered = lax.all_gather(mixed_b, "rows", axis=0, tiled=True)
    values = jnp.einsum(
        "nk,mblko->blnom",
        own_table,
        gathered.astype(jnp.float32),
        precision=high,
    )
    back_b = values.astype(jnp.bfloat16)

    def finish(pair):
        grid, coarse = pair
        spectral = jnp.dot(
            coarse.reshape(-1, lon_modes), lon_table.T, preferred_element_type=jnp.float32
        )
        spectral = spectral.reshape(lat_rows, chans, lon_cells)
        local = jnp.einsum("co,ncx->nox", local_weight, grid, preferred_element_type=jnp.float32)
        value = spectral + local + local_bias[None, :, None]
        act = jax.nn.gelu(value, approximate=False).astype(jnp.bfloat16)
        gate = jnp.einsum("ch,ncx->nhx", gate_weight, act, preferred_element_type=jnp.float32)
        upper = jnp.einsum("ch,ncx->nhx", up_weight, act, preferred_element_type=jnp.float32)
        hidden = (jax.nn.silu(gate) * upper).astype(jnp.bfloat16)
        down = jnp.einsum("hc,nhx->ncx", down_weight, hidden, preferred_element_type=jnp.float32)
        return (grid.astype(jnp.float32) + down).astype(jnp.bfloat16)

    result = lax.map(
        finish,
        (
            field.reshape(batch * levels, lat_rows, chans, lon_cells),
            back_b.reshape(batch * levels, lat_rows, chans, lon_modes),
        ),
    )
    return result.reshape(batch, levels, lat_rows, chans, lon_cells)


def solution(mesh):
    return jax.shard_map(
        body,
        mesh=mesh,
        in_specs=(
            P(None, "lev", "rows", None, None),
            P(None, None, "rows", None, None),
            P(),
            P(),
            P(),
            P(),
            P(),
        ),
        out_specs=P(None, "lev", "rows", None, None),
        check_vma=False,
    )
```

```python
import math

import jax
import jax.numpy as jnp
from jax import lax
from jax.sharding import PartitionSpec as P


def extended(cells, sides, width):
    for axis, dim in sides:
        count = lax.axis_size(axis)
        ends = count - 1
        head = lax.slice_in_dim(cells, 0, width, axis=dim)
        tail = lax.slice_in_dim(cells, cells.shape[dim] - width, cells.shape[dim], axis=dim)
        cells = jnp.concatenate(
            [
                lax.ppermute(tail, axis, [(i, (i + 1) % count) for i in range(ends)]),
                cells,
                lax.ppermute(head, axis, [((i + 1) % count, i) for i in range(ends)]),
            ],
            axis=dim,
        )
    return cells


def cas_rows(positions, count, modes):
    freq = jnp.arange(modes, dtype=jnp.int32) - modes // 2
    turns = positions[:, None] * freq[None, :] % count
    angle = 2.0 * math.pi / count * turns.astype(jnp.float32)
    return (jnp.cos(angle) + jnp.sin(angle)) / math.sqrt(count)


def body(field, spectral_weight, local_weight, local_bias, gate_weight, up_weight, down_weight):
    high = lax.Precision.HIGHEST
    batch, levels, lat_rows, chans, lon_cells = field.shape
    ranks = lax.axis_size("rows")
    lat_total = lat_rows * ranks
    lat_modes = spectral_weight.shape[1]
    lon_modes = spectral_weight.shape[2] * ranks
    lon_table = cas_rows(jnp.arange(lon_cells, dtype=jnp.int32), lon_cells, lon_modes).astype(
        jnp.bfloat16
    )
    own_rows = lax.axis_index("rows") * lat_rows + jnp.arange(lat_rows, dtype=jnp.int32)
    own_table = cas_rows(own_rows, lat_total, lat_modes)
    along = jnp.einsum("xm,blncx->mblnc", lon_table, field, preferred_element_type=jnp.float32)
    partial_modes = jnp.einsum("nk,mblnc->mblkc", own_table, along, precision=high)
    per = lon_modes // ranks
    pieces = partial_modes.astype(jnp.bfloat16).reshape((ranks, per) + partial_modes.shape[1:])
    pieces = lax.all_to_all(pieces, "rows", 0, 0, tiled=True)
    modes = pieces.astype(jnp.float32).sum(0).astype(jnp.bfloat16)
    padded = extended(modes, (("lev", 2),), 1)
    mixed = jnp.einsum(
        "kjco,jblkc->jblko",
        spectral_weight[0],
        padded[:, :, 0:levels],
        preferred_element_type=jnp.float32,
    )
    mixed = mixed + jnp.einsum(
        "kjco,jblkc->jblko",
        spectral_weight[1],
        padded[:, :, 1 : levels + 1],
        preferred_element_type=jnp.float32,
    )
    mixed = mixed + jnp.einsum(
        "kjco,jblkc->jblko",
        spectral_weight[2],
        padded[:, :, 2 : levels + 2],
        preferred_element_type=jnp.float32,
    )
    mixed_b = mixed.astype(jnp.bfloat16)
    copies = jnp.broadcast_to(mixed_b[None], (ranks,) + mixed_b.shape)
    gathered = lax.all_to_all(copies, "rows", 0, 0, tiled=True).reshape(
        (lon_modes,) + mixed_b.shape[1:]
    )
    values = jnp.einsum(
        "nk,mblko->blnom",
        own_table,
        gathered.astype(jnp.float32),
        precision=high,
    )
    back_b = values.astype(jnp.bfloat16)

    def finish(pair):
        grid, coarse = pair
        spectral = jnp.dot(
            coarse.reshape(-1, lon_modes), lon_table.T, preferred_element_type=jnp.float32
        )
        spectral = spectral.reshape(lat_rows, chans, lon_cells)
        local = jnp.einsum("co,ncx->nox", local_weight, grid, preferred_element_type=jnp.float32)
        value = spectral + local + local_bias[None, :, None]
        act = jax.nn.gelu(value, approximate=False).astype(jnp.bfloat16)
        gate = jnp.einsum("ch,ncx->nhx", gate_weight, act, preferred_element_type=jnp.float32)
        upper = jnp.einsum("ch,ncx->nhx", up_weight, act, preferred_element_type=jnp.float32)
        hidden = (jax.nn.silu(gate) * upper).astype(jnp.bfloat16)
        down = jnp.einsum("hc,nhx->ncx", down_weight, hidden, preferred_element_type=jnp.float32)
        return (grid.astype(jnp.float32) + down).astype(jnp.bfloat16)

    result = lax.map(
        finish,
        (
            field.reshape(batch * levels, lat_rows, chans, lon_cells),
            back_b.reshape(batch * levels, lat_rows, chans, lon_modes),
        ),
    )
    return result.reshape(batch, levels, lat_rows, chans, lon_cells)


def solution(mesh):
    return jax.shard_map(
        body,
        mesh=mesh,
        in_specs=(
            P(None, "lev", "rows", None, None),
            P(None, None, "rows", None, None),
            P(),
            P(),
            P(),
            P(),
            P(),
        ),
        out_specs=P(None, "lev", "rows", None, None),
        check_vma=False,
    )
```

```python
import math

import jax
import jax.numpy as jnp
from jax import lax
from jax.experimental import pallas as pl
from jax.experimental.pallas import tpu as pltpu
from jax.sharding import PartitionSpec as P


def extended(cells, sides, width):
    for axis, dim in sides:
        count = lax.axis_size(axis)
        ends = count - 1
        head = lax.slice_in_dim(cells, 0, width, axis=dim)
        tail = lax.slice_in_dim(cells, cells.shape[dim] - width, cells.shape[dim], axis=dim)
        cells = jnp.concatenate(
            [
                lax.ppermute(tail, axis, [(i, (i + 1) % count) for i in range(ends)]),
                cells,
                lax.ppermute(head, axis, [((i + 1) % count, i) for i in range(ends)]),
            ],
            axis=dim,
        )
    return cells


def cas_rows(positions, count, modes):
    freq = jnp.arange(modes, dtype=jnp.int32) - modes // 2
    turns = positions[:, None] * freq[None, :] % count
    angle = 2.0 * math.pi / count * turns.astype(jnp.float32)
    return (jnp.cos(angle) + jnp.sin(angle)) / math.sqrt(count)


def finish_kernel(field_ref, back_ref, lon_ref, local_ref, bias_ref, gate_ref, up_ref, down_ref, out_ref):
    sqrt_half = math.sqrt(0.5)
    for r in range(field_ref.shape[0]):
        grid = field_ref[r]
        spectral = jnp.dot(back_ref[r], lon_ref[...], preferred_element_type=jnp.float32)
        local = jnp.dot(local_ref[...], grid, preferred_element_type=jnp.float32)
        value = spectral + local + bias_ref[...]
        act = (0.5 * value * (1.0 + lax.erf(value * sqrt_half))).astype(jnp.bfloat16)
        gate = jnp.dot(gate_ref[...], act, preferred_element_type=jnp.float32)
        upper = jnp.dot(up_ref[...], act, preferred_element_type=jnp.float32)
        hidden = (gate / (1.0 + jnp.exp(-gate)) * upper).astype(jnp.bfloat16)
        down = jnp.dot(down_ref[...], hidden, preferred_element_type=jnp.float32)
        out_ref[r] = (grid.astype(jnp.float32) + down).astype(out_ref.dtype)


def finish(field, back, lon_table, local_weight, local_bias, gate_weight, up_weight, down_weight, block=2):
    rows, chans, lon_cells = field.shape
    modes = back.shape[2]
    hid = gate_weight.shape[1]
    whole = lambda i: (0, 0)
    return pl.pallas_call(
        finish_kernel,
        out_shape=jax.ShapeDtypeStruct(field.shape, field.dtype),
        grid=(rows // block,),
        in_specs=[
            pl.BlockSpec((block, chans, lon_cells), lambda i: (i, 0, 0)),
            pl.BlockSpec((block, chans, modes), lambda i: (i, 0, 0)),
            pl.BlockSpec((modes, lon_cells), whole),
            pl.BlockSpec((chans, chans), whole),
            pl.BlockSpec((chans, 1), whole),
            pl.BlockSpec((hid, chans), whole),
            pl.BlockSpec((hid, chans), whole),
            pl.BlockSpec((chans, hid), whole),
        ],
        out_specs=pl.BlockSpec((block, chans, lon_cells), lambda i: (i, 0, 0)),
        cost_estimate=pl.CostEstimate(
            flops=2 * rows * lon_cells * chans * (modes + chans + 3 * hid),
            transcendentals=rows * lon_cells * (chans + 2 * hid),
            bytes_accessed=4 * field.size + 2 * back.size,
        ),
    )(
        field,
        back,
        lon_table.T,
        local_weight.T,
        local_bias.reshape(chans, 1),
        gate_weight.T,
        up_weight.T,
        down_weight.T,
    )


def body(field, spectral_weight, local_weight, local_bias, gate_weight, up_weight, down_weight):
    high = lax.Precision.HIGHEST
    batch, levels, lat_rows, chans, lon_cells = field.shape
    ranks = lax.axis_size("rows")
    lat_total = lat_rows * ranks
    lat_modes = spectral_weight.shape[1]
    lon_modes = spectral_weight.shape[2] * ranks
    lon_table = cas_rows(jnp.arange(lon_cells, dtype=jnp.int32), lon_cells, lon_modes).astype(
        jnp.bfloat16
    )
    own_rows = lax.axis_index("rows") * lat_rows + jnp.arange(lat_rows, dtype=jnp.int32)
    own_table = cas_rows(own_rows, lat_total, lat_modes)
    along = jnp.einsum("xm,blncx->mblnc", lon_table, field, preferred_element_type=jnp.float32)
    partial_modes = jnp.einsum("nk,mblnc->mblkc", own_table, along, precision=high)
    per = lon_modes // ranks
    pieces = partial_modes.astype(jnp.bfloat16).reshape((ranks, per) + partial_modes.shape[1:])
    pieces = lax.all_to_all(pieces, "rows", 0, 0, tiled=True)
    modes = pieces.astype(jnp.float32).sum(0).astype(jnp.bfloat16)
    padded = extended(modes, (("lev", 2),), 1)
    mixed = jnp.einsum(
        "kjco,jblkc->jblko",
        spectral_weight[0],
        padded[:, :, 0:levels],
        preferred_element_type=jnp.float32,
    )
    mixed = mixed + jnp.einsum(
        "kjco,jblkc->jblko",
        spectral_weight[1],
        padded[:, :, 1 : levels + 1],
        preferred_element_type=jnp.float32,
    )
    mixed = mixed + jnp.einsum(
        "kjco,jblkc->jblko",
        spectral_weight[2],
        padded[:, :, 2 : levels + 2],
        preferred_element_type=jnp.float32,
    )
    mixed_b = mixed.astype(jnp.bfloat16)
    copies = jnp.broadcast_to(mixed_b[None], (ranks,) + mixed_b.shape)
    gathered = lax.all_to_all(copies, "rows", 0, 0, tiled=True).reshape(
        (lon_modes,) + mixed_b.shape[1:]
    )
    values = jnp.einsum(
        "nk,mblko->blnom",
        own_table,
        gathered.astype(jnp.float32),
        precision=high,
    )
    back_b = values.astype(jnp.bfloat16)

    result = finish(
        field.reshape(batch * levels * lat_rows, chans, lon_cells),
        back_b.reshape(batch * levels * lat_rows, chans, lon_modes),
        lon_table,
        local_weight,
        local_bias,
        gate_weight,
        up_weight,
        down_weight,
    )
    return result.reshape(batch, levels, lat_rows, chans, lon_cells)


def solution(mesh):
    return jax.shard_map(
        body,
        mesh=mesh,
        in_specs=(
            P(None, "lev", "rows", None, None),
            P(None, None, "rows", None, None),
            P(),
            P(),
            P(),
            P(),
            P(),
        ),
        out_specs=P(None, "lev", "rows", None, None),
        check_vma=False,
    )
```

```python
import math

import jax
import jax.numpy as jnp
from jax import lax
from jax.experimental import pallas as pl
from jax.experimental.pallas import tpu as pltpu
from jax.sharding import PartitionSpec as P


def extended(cells, sides, width):
    for axis, dim in sides:
        count = lax.axis_size(axis)
        ends = count - 1
        head = lax.slice_in_dim(cells, 0, width, axis=dim)
        tail = lax.slice_in_dim(cells, cells.shape[dim] - width, cells.shape[dim], axis=dim)
        cells = jnp.concatenate(
            [
                lax.ppermute(tail, axis, [(i, (i + 1) % count) for i in range(ends)]),
                cells,
                lax.ppermute(head, axis, [((i + 1) % count, i) for i in range(ends)]),
            ],
            axis=dim,
        )
    return cells


def cas_rows(positions, count, modes):
    freq = jnp.arange(modes, dtype=jnp.int32) - modes // 2
    turns = positions[:, None] * freq[None, :] % count
    angle = 2.0 * math.pi / count * turns.astype(jnp.float32)
    return (jnp.cos(angle) + jnp.sin(angle)) / math.sqrt(count)


def finish_kernel(field_ref, back_ref, lon_ref, local_ref, bias_ref, gate_ref, up_ref, down_ref, out_ref):
    sqrt_half = math.sqrt(0.5)
    for r in range(field_ref.shape[0]):
        grid = field_ref[r]
        spectral = jnp.dot(back_ref[r], lon_ref[...], preferred_element_type=jnp.float32)
        local = jnp.dot(local_ref[...], grid, preferred_element_type=jnp.float32)
        value = spectral + local + bias_ref[...]
        act = (0.5 * value * (1.0 + lax.erf(value * sqrt_half))).astype(jnp.bfloat16)
        gate = jnp.dot(gate_ref[...], act, preferred_element_type=jnp.float32)
        upper = jnp.dot(up_ref[...], act, preferred_element_type=jnp.float32)
        hidden = (gate / (1.0 + jnp.exp(-gate)) * upper).astype(jnp.bfloat16)
        down = jnp.dot(down_ref[...], hidden, preferred_element_type=jnp.float32)
        out_ref[r] = (grid.astype(jnp.float32) + down).astype(out_ref.dtype)


def finish(field, back, lon_table, local_weight, local_bias, gate_weight, up_weight, down_weight, block=2):
    rows, chans, lon_cells = field.shape
    modes = back.shape[2]
    hid = gate_weight.shape[1]
    whole = lambda i: (0, 0)
    return pl.pallas_call(
        finish_kernel,
        out_shape=jax.ShapeDtypeStruct(field.shape, field.dtype),
        grid=(rows // block,),
        in_specs=[
            pl.BlockSpec((block, chans, lon_cells), lambda i: (i, 0, 0)),
            pl.BlockSpec((block, chans, modes), lambda i: (i, 0, 0)),
            pl.BlockSpec((modes, lon_cells), whole),
            pl.BlockSpec((chans, chans), whole),
            pl.BlockSpec((chans, 1), whole),
            pl.BlockSpec((hid, chans), whole),
            pl.BlockSpec((hid, chans), whole),
            pl.BlockSpec((chans, hid), whole),
        ],
        out_specs=pl.BlockSpec((block, chans, lon_cells), lambda i: (i, 0, 0)),
        cost_estimate=pl.CostEstimate(
            flops=2 * rows * lon_cells * chans * (modes + chans + 3 * hid),
            transcendentals=rows * lon_cells * (chans + 2 * hid),
            bytes_accessed=4 * field.size + 2 * back.size,
        ),
    )(
        field,
        back,
        lon_table.T,
        local_weight.T,
        local_bias.reshape(chans, 1),
        gate_weight.T,
        up_weight.T,
        down_weight.T,
    )


def body(field, spectral_weight, local_weight, local_bias, gate_weight, up_weight, down_weight):
    high = lax.Precision.HIGHEST
    batch, levels, lat_rows, chans, lon_cells = field.shape
    ranks = lax.axis_size("rows")
    lat_total = lat_rows * ranks
    lat_modes = spectral_weight.shape[1]
    lon_modes = spectral_weight.shape[2] * ranks
    lon_table = cas_rows(jnp.arange(lon_cells, dtype=jnp.int32), lon_cells, lon_modes).astype(
        jnp.bfloat16
    )
    lat_table = cas_rows(jnp.arange(lat_total, dtype=jnp.int32), lat_total, lat_modes).reshape(
        ranks, lat_rows, lat_modes
    )
    per = lon_modes // ranks
    along = jnp.einsum("xm,blncx->mblnc", lon_table, field, preferred_element_type=jnp.float32)
    along = lax.all_to_all(along.reshape((ranks, per) + along.shape[1:]), "rows", 0, 0, tiled=True)
    modes = jnp.einsum("sjblnc,snk->jblkc", along, lat_table, precision=high)
    modes = modes.astype(jnp.bfloat16)
    padded = extended(modes, (("lev", 2),), 1)
    mixed = jnp.einsum(
        "kjco,jblkc->jblko",
        spectral_weight[0],
        padded[:, :, 0:levels],
        preferred_element_type=jnp.float32,
    )
    mixed = mixed + jnp.einsum(
        "kjco,jblkc->jblko",
        spectral_weight[1],
        padded[:, :, 1 : levels + 1],
        preferred_element_type=jnp.float32,
    )
    mixed = mixed + jnp.einsum(
        "kjco,jblkc->jblko",
        spectral_weight[2],
        padded[:, :, 2 : levels + 2],
        preferred_element_type=jnp.float32,
    )
    mixed_b = mixed.astype(jnp.bfloat16)
    values = jnp.einsum(
        "rnk,jblko->rjblno", lat_table, mixed_b.astype(jnp.float32), precision=high
    )
    values = lax.all_to_all(values.astype(jnp.bfloat16), "rows", 0, 0, tiled=True)
    back_b = jnp.transpose(values, (2, 3, 4, 5, 0, 1)).reshape(
        batch, levels, lat_rows, chans, lon_modes
    )

    result = finish(
        field.reshape(batch * levels * lat_rows, chans, lon_cells),
        back_b.reshape(batch * levels * lat_rows, chans, lon_modes),
        lon_table,
        local_weight,
        local_bias,
        gate_weight,
        up_weight,
        down_weight,
    )
    return result.reshape(batch, levels, lat_rows, chans, lon_cells)


def solution(mesh):
    return jax.shard_map(
        body,
        mesh=mesh,
        in_specs=(
            P(None, "lev", "rows", None, None),
            P(None, None, "rows", None, None),
            P(),
            P(),
            P(),
            P(),
            P(),
        ),
        out_specs=P(None, "lev", "rows", None, None),
        check_vma=False,
    )
```

```python
import functools
import math

import jax
import jax.numpy as jnp
from jax import lax
from jax.experimental import pallas as pl
from jax.experimental.pallas import tpu as pltpu
from jax.sharding import PartitionSpec as P


def extended(cells, sides, width):
    for axis, dim in sides:
        count = lax.axis_size(axis)
        ends = count - 1
        head = lax.slice_in_dim(cells, 0, width, axis=dim)
        tail = lax.slice_in_dim(cells, cells.shape[dim] - width, cells.shape[dim], axis=dim)
        cells = jnp.concatenate(
            [
                lax.ppermute(tail, axis, [(i, (i + 1) % count) for i in range(ends)]),
                cells,
                lax.ppermute(head, axis, [((i + 1) % count, i) for i in range(ends)]),
            ],
            axis=dim,
        )
    return cells


def cas_rows(positions, count, modes):
    freq = jnp.arange(modes, dtype=jnp.int32) - modes // 2
    turns = positions[:, None] * freq[None, :] % count
    angle = 2.0 * math.pi / count * turns.astype(jnp.float32)
    return (jnp.cos(angle) + jnp.sin(angle)) / math.sqrt(count)


def exchange_kernel(axis, x_ref, y_ref, send_sems, recv_sems, own_sem):
    ranks = x_ref.shape[0]
    me = lax.axis_index(axis)
    barrier = pltpu.get_barrier_semaphore()

    def greet(i, carry):
        peer = lax.rem(me + i, ranks)
        pl.semaphore_signal(
            barrier, inc=1, device_id={axis: peer}, device_id_type=pl.DeviceIdType.MESH
        )
        return carry

    lax.fori_loop(1, ranks, greet, 0)
    pl.semaphore_wait(barrier, ranks - 1)

    own = pltpu.make_async_copy(x_ref.at[me], y_ref.at[me], own_sem)
    own.start()

    def copy_to(peer):
        return pltpu.make_async_remote_copy(
            src_ref=x_ref.at[peer],
            dst_ref=y_ref.at[me],
            send_sem=send_sems.at[peer],
            recv_sem=recv_sems.at[me],
            device_id={axis: peer},
            device_id_type=pl.DeviceIdType.MESH,
        )

    def send(i, carry):
        copy_to(lax.rem(me + i, ranks)).start()
        return carry

    lax.fori_loop(1, ranks, send, 0)

    def wait(i, carry):
        copy_to(lax.rem(me + i, ranks)).wait_send()
        source = lax.rem(me + ranks - i, ranks)
        pltpu.make_async_remote_copy(
            src_ref=x_ref.at[source],
            dst_ref=y_ref.at[source],
            send_sem=send_sems.at[source],
            recv_sem=recv_sems.at[source],
            device_id={axis: source},
            device_id_type=pl.DeviceIdType.MESH,
        ).wait_recv()
        return carry

    lax.fori_loop(1, ranks, wait, 0)
    own.wait()


def exchange(x, axis, collective_id):
    ranks = x.shape[0]
    return pl.pallas_call(
        functools.partial(exchange_kernel, axis),
        out_shape=jax.ShapeDtypeStruct(x.shape, x.dtype),
        in_specs=[pl.BlockSpec(memory_space=pl.ANY)],
        out_specs=pl.BlockSpec(memory_space=pl.ANY),
        scratch_shapes=[
            pltpu.SemaphoreType.DMA((ranks,)),
            pltpu.SemaphoreType.DMA((ranks,)),
            pltpu.SemaphoreType.DMA,
        ],
        compiler_params=pltpu.CompilerParams(collective_id=collective_id, has_side_effects=True),
    )(x)


def finish_kernel(field_ref, back_ref, lon_ref, local_ref, bias_ref, gate_ref, up_ref, down_ref, out_ref):
    sqrt_half = math.sqrt(0.5)
    for r in range(field_ref.shape[0]):
        grid = field_ref[r]
        spectral = jnp.dot(back_ref[r], lon_ref[...], preferred_element_type=jnp.float32)
        local = jnp.dot(local_ref[...], grid, preferred_element_type=jnp.float32)
        value = spectral + local + bias_ref[...]
        act = (0.5 * value * (1.0 + lax.erf(value * sqrt_half))).astype(jnp.bfloat16)
        gate = jnp.dot(gate_ref[...], act, preferred_element_type=jnp.float32)
        upper = jnp.dot(up_ref[...], act, preferred_element_type=jnp.float32)
        hidden = (gate / (1.0 + jnp.exp(-gate)) * upper).astype(jnp.bfloat16)
        down = jnp.dot(down_ref[...], hidden, preferred_element_type=jnp.float32)
        out_ref[r] = (grid.astype(jnp.float32) + down).astype(out_ref.dtype)


def finish(field, back, lon_table, local_weight, local_bias, gate_weight, up_weight, down_weight, block=2):
    rows, chans, lon_cells = field.shape
    modes = back.shape[2]
    hid = gate_weight.shape[1]
    whole = lambda i: (0, 0)
    return pl.pallas_call(
        finish_kernel,
        out_shape=jax.ShapeDtypeStruct(field.shape, field.dtype),
        grid=(rows // block,),
        in_specs=[
            pl.BlockSpec((block, chans, lon_cells), lambda i: (i, 0, 0)),
            pl.BlockSpec((block, chans, modes), lambda i: (i, 0, 0)),
            pl.BlockSpec((modes, lon_cells), whole),
            pl.BlockSpec((chans, chans), whole),
            pl.BlockSpec((chans, 1), whole),
            pl.BlockSpec((hid, chans), whole),
            pl.BlockSpec((hid, chans), whole),
            pl.BlockSpec((chans, hid), whole),
        ],
        out_specs=pl.BlockSpec((block, chans, lon_cells), lambda i: (i, 0, 0)),
        cost_estimate=pl.CostEstimate(
            flops=2 * rows * lon_cells * chans * (modes + chans + 3 * hid),
            transcendentals=rows * lon_cells * (chans + 2 * hid),
            bytes_accessed=4 * field.size + 2 * back.size,
        ),
    )(
        field,
        back,
        lon_table.T,
        local_weight.T,
        local_bias.reshape(chans, 1),
        gate_weight.T,
        up_weight.T,
        down_weight.T,
    )


def body(field, spectral_weight, local_weight, local_bias, gate_weight, up_weight, down_weight):
    high = lax.Precision.HIGHEST
    batch, levels, lat_rows, chans, lon_cells = field.shape
    ranks = lax.axis_size("rows")
    lat_total = lat_rows * ranks
    lat_modes = spectral_weight.shape[1]
    lon_modes = spectral_weight.shape[2] * ranks
    lon_table = cas_rows(jnp.arange(lon_cells, dtype=jnp.int32), lon_cells, lon_modes).astype(
        jnp.bfloat16
    )
    lat_table = cas_rows(jnp.arange(lat_total, dtype=jnp.int32), lat_total, lat_modes).reshape(
        ranks, lat_rows, lat_modes
    )
    per = lon_modes // ranks
    along = jnp.einsum("xm,blncx->mblnc", lon_table, field, preferred_element_type=jnp.float32)
    along = exchange(along.reshape((ranks, per) + along.shape[1:]), "rows", 0)
    modes = jnp.einsum("sjblnc,snk->jblkc", along, lat_table, precision=high)
    modes = modes.astype(jnp.bfloat16)
    padded = extended(modes, (("lev", 2),), 1)
    mixed = jnp.einsum(
        "kjco,jblkc->jblko",
        spectral_weight[0],
        padded[:, :, 0:levels],
        preferred_element_type=jnp.float32,
    )
    mixed = mixed + jnp.einsum(
        "kjco,jblkc->jblko",
        spectral_weight[1],
        padded[:, :, 1 : levels + 1],
        preferred_element_type=jnp.float32,
    )
    mixed = mixed + jnp.einsum(
        "kjco,jblkc->jblko",
        spectral_weight[2],
        padded[:, :, 2 : levels + 2],
        preferred_element_type=jnp.float32,
    )
    mixed_b = mixed.astype(jnp.bfloat16)
    values = jnp.einsum(
        "rnk,jblko->rjblno", lat_table, mixed_b.astype(jnp.float32), precision=high
    )
    values = exchange(values.astype(jnp.bfloat16), "rows", 1)
    back_b = jnp.transpose(values, (2, 3, 4, 5, 0, 1)).reshape(
        batch, levels, lat_rows, chans, lon_modes
    )

    result = finish(
        field.reshape(batch * levels * lat_rows, chans, lon_cells),
        back_b.reshape(batch * levels * lat_rows, chans, lon_modes),
        lon_table,
        local_weight,
        local_bias,
        gate_weight,
        up_weight,
        down_weight,
    )
    return result.reshape(batch, levels, lat_rows, chans, lon_cells)


def solution(mesh):
    return jax.shard_map(
        body,
        mesh=mesh,
        in_specs=(
            P(None, "lev", "rows", None, None),
            P(None, None, "rows", None, None),
            P(),
            P(),
            P(),
            P(),
            P(),
        ),
        out_specs=P(None, "lev", "rows", None, None),
        check_vma=False,
    )
```

```python
import math

import jax
import jax.numpy as jnp
from jax import lax
from jax.experimental import pallas as pl
from jax.experimental.pallas import tpu as pltpu
from jax.sharding import PartitionSpec as P


def extended(cells, sides, width):
    for axis, dim in sides:
        count = lax.axis_size(axis)
        ends = count - 1
        head = lax.slice_in_dim(cells, 0, width, axis=dim)
        tail = lax.slice_in_dim(cells, cells.shape[dim] - width, cells.shape[dim], axis=dim)
        cells = jnp.concatenate(
            [
                lax.ppermute(tail, axis, [(i, (i + 1) % count) for i in range(ends)]),
                cells,
                lax.ppermute(head, axis, [((i + 1) % count, i) for i in range(ends)]),
            ],
            axis=dim,
        )
    return cells


def cas_rows(positions, count, modes):
    freq = jnp.arange(modes, dtype=jnp.int32) - modes // 2
    turns = positions[:, None] * freq[None, :] % count
    angle = 2.0 * math.pi / count * turns.astype(jnp.float32)
    return (jnp.cos(angle) + jnp.sin(angle)) / math.sqrt(count)


def finish_kernel(field_ref, back_ref, lon_ref, local_ref, bias_ref, gate_ref, up_ref, down_ref, *rest):
    out_ref = rest[-1]
    sqrt_half = math.sqrt(0.5)
    for r in range(field_ref.shape[0]):
        grid = field_ref[r]
        spectral = jnp.dot(back_ref[r], lon_ref[...], preferred_element_type=jnp.float32)
        local = jnp.dot(local_ref[...], grid, preferred_element_type=jnp.float32)
        value = spectral + local + bias_ref[...]
        act = (0.5 * value * (1.0 + lax.erf(value * sqrt_half))).astype(jnp.bfloat16)
        gate = jnp.dot(gate_ref[...], act, preferred_element_type=jnp.float32)
        upper = jnp.dot(up_ref[...], act, preferred_element_type=jnp.float32)
        hidden = (gate / (1.0 + jnp.exp(-gate)) * upper).astype(jnp.bfloat16)
        down = jnp.dot(down_ref[...], hidden, preferred_element_type=jnp.float32)
        out_ref[r] = (grid.astype(jnp.float32) + down).astype(out_ref.dtype)


def finish(field, back, lon_table, local_weight, local_bias, gate_weight, up_weight, down_weight, start, prev=None, block=2):
    rows, chans, lon_cells = field.shape
    part, _, modes = back.shape
    hid = gate_weight.shape[1]
    whole = lambda i: (0, 0)
    shift = start // block
    in_specs = [
        pl.BlockSpec((block, chans, lon_cells), lambda i: (i + shift, 0, 0)),
        pl.BlockSpec((block, chans, modes), lambda i: (i, 0, 0)),
        pl.BlockSpec((modes, lon_cells), whole),
        pl.BlockSpec((chans, chans), whole),
        pl.BlockSpec((chans, 1), whole),
        pl.BlockSpec((hid, chans), whole),
        pl.BlockSpec((hid, chans), whole),
        pl.BlockSpec((chans, hid), whole),
    ]
    args = [
        field,
        back,
        lon_table.T,
        local_weight.T,
        local_bias.reshape(chans, 1),
        gate_weight.T,
        up_weight.T,
        down_weight.T,
    ]
    aliases = {}
    if prev is not None:
        in_specs.append(pl.BlockSpec(memory_space=pl.ANY))
        args.append(prev)
        aliases = {len(args) - 1: 0}
    return pl.pallas_call(
        finish_kernel,
        out_shape=jax.ShapeDtypeStruct(field.shape, field.dtype),
        grid=(part // block,),
        in_specs=in_specs,
        out_specs=pl.BlockSpec((block, chans, lon_cells), lambda i: (i + shift, 0, 0)),
        input_output_aliases=aliases,
        cost_estimate=pl.CostEstimate(
            flops=2 * part * lon_cells * chans * (modes + chans + 3 * hid),
            transcendentals=part * lon_cells * (chans + 2 * hid),
            bytes_accessed=4 * part * chans * lon_cells + 2 * back.size,
        ),
    )(*args)


def body(field, spectral_weight, local_weight, local_bias, gate_weight, up_weight, down_weight):
    high = lax.Precision.HIGHEST
    batch, levels, lat_rows, chans, lon_cells = field.shape
    ranks = lax.axis_size("rows")
    lat_total = lat_rows * ranks
    lat_modes = spectral_weight.shape[1]
    lon_modes = spectral_weight.shape[2] * ranks
    lon_table = cas_rows(jnp.arange(lon_cells, dtype=jnp.int32), lon_cells, lon_modes).astype(
        jnp.bfloat16
    )
    lat_table = cas_rows(jnp.arange(lat_total, dtype=jnp.int32), lat_total, lat_modes).reshape(
        ranks, lat_rows, lat_modes
    )
    per = lon_modes // ranks

    def synthesis(grid):
        along = jnp.einsum("xm,blncx->mblnc", lon_table, grid, preferred_element_type=jnp.float32)
        along = lax.all_to_all(
            along.reshape((ranks, per) + along.shape[1:]), "rows", 0, 0, tiled=True
        )
        modes = jnp.einsum("sjblnc,snk->jblkc", along, lat_table, precision=high)
        modes = modes.astype(jnp.bfloat16)
        padded = extended(modes, (("lev", 2),), 1)
        mixed = jnp.einsum(
            "kjco,jblkc->jblko",
            spectral_weight[0],
            padded[:, :, 0:levels],
            preferred_element_type=jnp.float32,
        )
        mixed = mixed + jnp.einsum(
            "kjco,jblkc->jblko",
            spectral_weight[1],
            padded[:, :, 1 : levels + 1],
            preferred_element_type=jnp.float32,
        )
        mixed = mixed + jnp.einsum(
            "kjco,jblkc->jblko",
            spectral_weight[2],
            padded[:, :, 2 : levels + 2],
            preferred_element_type=jnp.float32,
        )
        mixed_b = mixed.astype(jnp.bfloat16)
        values = jnp.einsum(
            "rnk,jblko->rjblno", lat_table, mixed_b.astype(jnp.float32), precision=high
        )
        return values.astype(jnp.bfloat16)

    def arrive(values):
        values = lax.all_to_all(values, "rows", 0, 0, tiled=True)
        back_b = jnp.transpose(values, (2, 3, 4, 5, 0, 1))
        return back_b.reshape(-1, chans, lon_modes)

    rows = field.reshape(batch * levels * lat_rows, chans, lon_cells)
    result = None
    sent = [synthesis(field[0:1])]
    for sample in range(batch):
        back_b = arrive(sent[sample])
        if sample + 1 < batch:
            following = synthesis(field[sample + 1 : sample + 2])
            back_b, following = lax.optimization_barrier((back_b, following))
            sent.append(following)
        result = finish(
            rows,
            back_b,
            lon_table,
            local_weight,
            local_bias,
            gate_weight,
            up_weight,
            down_weight,
            sample * levels * lat_rows,
            result,
        )
    return result.reshape(batch, levels, lat_rows, chans, lon_cells)


def solution(mesh):
    return jax.shard_map(
        body,
        mesh=mesh,
        in_specs=(
            P(None, "lev", "rows", None, None),
            P(None, None, "rows", None, None),
            P(),
            P(),
            P(),
            P(),
            P(),
        ),
        out_specs=P(None, "lev", "rows", None, None),
        check_vma=False,
    )
```

```python
import math

import jax
import jax.numpy as jnp
from jax import lax
from jax.experimental import pallas as pl
from jax.experimental.pallas import tpu as pltpu
from jax.sharding import PartitionSpec as P


def extended(cells, sides, width):
    for axis, dim in sides:
        count = lax.axis_size(axis)
        ends = count - 1
        head = lax.slice_in_dim(cells, 0, width, axis=dim)
        tail = lax.slice_in_dim(cells, cells.shape[dim] - width, cells.shape[dim], axis=dim)
        cells = jnp.concatenate(
            [
                lax.ppermute(tail, axis, [(i, (i + 1) % count) for i in range(ends)]),
                cells,
                lax.ppermute(head, axis, [((i + 1) % count, i) for i in range(ends)]),
            ],
            axis=dim,
        )
    return cells


def cas_rows(positions, count, modes):
    freq = jnp.arange(modes, dtype=jnp.int32) - modes // 2
    turns = positions[:, None] * freq[None, :] % count
    angle = 2.0 * math.pi / count * turns.astype(jnp.float32)
    return (jnp.cos(angle) + jnp.sin(angle)) / math.sqrt(count)


def finish_kernel(field_ref, back_ref, lon_ref, local_ref, bias_ref, gate_ref, up_ref, down_ref, out_ref):
    sqrt_half = math.sqrt(0.5)
    rows, _, lon_cells = field_ref.shape
    acts = []
    for r in range(rows):
        lhs = jnp.concatenate([back_ref[r], local_ref[...]], axis=1)
        rhs = jnp.concatenate([lon_ref[...], field_ref[r]], axis=0)
        value = jnp.dot(lhs, rhs, preferred_element_type=jnp.float32) + bias_ref[...]
        acts.append((0.5 * value * (1.0 + lax.erf(value * sqrt_half))).astype(jnp.bfloat16))
    act = jnp.concatenate(acts, axis=1)
    gate = jnp.dot(gate_ref[...], act, preferred_element_type=jnp.float32)
    upper = jnp.dot(up_ref[...], act, preferred_element_type=jnp.float32)
    hidden = (0.5 * gate * (1.0 + jnp.tanh(0.5 * gate)) * upper).astype(jnp.bfloat16)
    down = jnp.dot(down_ref[...], hidden, preferred_element_type=jnp.float32)
    for r in range(rows):
        grid = field_ref[r].astype(jnp.float32)
        out_ref[r] = (grid + down[:, r * lon_cells : (r + 1) * lon_cells]).astype(out_ref.dtype)


def finish(field, back, lon_table, local_weight, local_bias, gate_weight, up_weight, down_weight, block=4):
    rows, chans, lon_cells = field.shape
    modes = back.shape[2]
    hid = gate_weight.shape[1]
    whole = lambda i: (0, 0)
    return pl.pallas_call(
        finish_kernel,
        out_shape=jax.ShapeDtypeStruct(field.shape, field.dtype),
        grid=(rows // block,),
        in_specs=[
            pl.BlockSpec((block, chans, lon_cells), lambda i: (i, 0, 0)),
            pl.BlockSpec((block, chans, modes), lambda i: (i, 0, 0)),
            pl.BlockSpec((modes, lon_cells), whole),
            pl.BlockSpec((chans, chans), whole),
            pl.BlockSpec((chans, 1), whole),
            pl.BlockSpec((hid, chans), whole),
            pl.BlockSpec((hid, chans), whole),
            pl.BlockSpec((chans, hid), whole),
        ],
        out_specs=pl.BlockSpec((block, chans, lon_cells), lambda i: (i, 0, 0)),
        cost_estimate=pl.CostEstimate(
            flops=2 * rows * lon_cells * chans * (modes + chans + 3 * hid),
            transcendentals=rows * lon_cells * (chans + 2 * hid),
            bytes_accessed=4 * field.size + 2 * back.size,
        ),
    )(
        field,
        back,
        lon_table.T,
        local_weight.T,
        local_bias.reshape(chans, 1),
        gate_weight.T,
        up_weight.T,
        down_weight.T,
    )


def body(field, spectral_weight, local_weight, local_bias, gate_weight, up_weight, down_weight):
    high = lax.Precision.HIGHEST
    batch, levels, lat_rows, chans, lon_cells = field.shape
    ranks = lax.axis_size("rows")
    lat_total = lat_rows * ranks
    lat_modes = spectral_weight.shape[1]
    lon_modes = spectral_weight.shape[2] * ranks
    lon_table = cas_rows(jnp.arange(lon_cells, dtype=jnp.int32), lon_cells, lon_modes).astype(
        jnp.bfloat16
    )
    lat_table = cas_rows(jnp.arange(lat_total, dtype=jnp.int32), lat_total, lat_modes).reshape(
        ranks, lat_rows, lat_modes
    )
    per = lon_modes // ranks
    along = jnp.einsum("xm,blncx->mblnc", lon_table, field, preferred_element_type=jnp.float32)
    along = lax.all_to_all(along.reshape((ranks, per) + along.shape[1:]), "rows", 0, 0, tiled=True)
    modes = jnp.einsum("sjblnc,snk->jblkc", along, lat_table, precision=high)
    modes = modes.astype(jnp.bfloat16)
    padded = extended(modes, (("lev", 2),), 1)
    mixed = jnp.einsum(
        "kjco,jblkc->jblko",
        spectral_weight[0],
        padded[:, :, 0:levels],
        preferred_element_type=jnp.float32,
    )
    mixed = mixed + jnp.einsum(
        "kjco,jblkc->jblko",
        spectral_weight[1],
        padded[:, :, 1 : levels + 1],
        preferred_element_type=jnp.float32,
    )
    mixed = mixed + jnp.einsum(
        "kjco,jblkc->jblko",
        spectral_weight[2],
        padded[:, :, 2 : levels + 2],
        preferred_element_type=jnp.float32,
    )
    mixed_b = mixed.astype(jnp.bfloat16)
    values = jnp.einsum(
        "rnk,jblko->rjblno", lat_table, mixed_b.astype(jnp.float32), precision=high
    )
    values = lax.all_to_all(values.astype(jnp.bfloat16), "rows", 0, 0, tiled=True)
    back_b = jnp.transpose(values, (2, 3, 4, 5, 0, 1)).reshape(
        batch, levels, lat_rows, chans, lon_modes
    )

    result = finish(
        field.reshape(batch * levels * lat_rows, chans, lon_cells),
        back_b.reshape(batch * levels * lat_rows, chans, lon_modes),
        lon_table,
        local_weight,
        local_bias,
        gate_weight,
        up_weight,
        down_weight,
    )
    return result.reshape(batch, levels, lat_rows, chans, lon_cells)


def solution(mesh):
    return jax.shard_map(
        body,
        mesh=mesh,
        in_specs=(
            P(None, "lev", "rows", None, None),
            P(None, None, "rows", None, None),
            P(),
            P(),
            P(),
            P(),
            P(),
        ),
        out_specs=P(None, "lev", "rows", None, None),
        check_vma=False,
    )
```

```python
import math

import jax
import jax.numpy as jnp
from jax import lax
from jax.experimental import pallas as pl
from jax.experimental.pallas import tpu as pltpu
from jax.sharding import PartitionSpec as P


def extended(cells, sides, width):
    for axis, dim in sides:
        count = lax.axis_size(axis)
        ends = count - 1
        head = lax.slice_in_dim(cells, 0, width, axis=dim)
        tail = lax.slice_in_dim(cells, cells.shape[dim] - width, cells.shape[dim], axis=dim)
        cells = jnp.concatenate(
            [
                lax.ppermute(tail, axis, [(i, (i + 1) % count) for i in range(ends)]),
                cells,
                lax.ppermute(head, axis, [((i + 1) % count, i) for i in range(ends)]),
            ],
            axis=dim,
        )
    return cells


def cas_rows(positions, count, modes):
    freq = jnp.arange(modes, dtype=jnp.int32) - modes // 2
    turns = positions[:, None] * freq[None, :] % count
    angle = 2.0 * math.pi / count * turns.astype(jnp.float32)
    return (jnp.cos(angle) + jnp.sin(angle)) / math.sqrt(count)


def finish_kernel(field_ref, back_ref, lon_ref, local_ref, bias_ref, gate_ref, up_ref, down_ref, out_ref):
    sqrt_half = math.sqrt(0.5)
    rows, _, lon_cells = field_ref.shape
    acts = []
    for r in range(rows):
        lhs = jnp.concatenate([back_ref[r], local_ref[...]], axis=1)
        rhs = jnp.concatenate([lon_ref[...], field_ref[r]], axis=0)
        value = jnp.dot(lhs, rhs, preferred_element_type=jnp.float32) + bias_ref[...]
        acts.append((0.5 * value * (1.0 + lax.erf(value * sqrt_half))).astype(jnp.bfloat16))
    act = jnp.concatenate(acts, axis=1)
    gate = jnp.dot(gate_ref[...], act, preferred_element_type=jnp.float32)
    upper = jnp.dot(up_ref[...], act, preferred_element_type=jnp.float32)
    hidden = (0.5 * gate * (1.0 + jnp.tanh(0.5 * gate)) * upper).astype(jnp.bfloat16)
    down = jnp.dot(down_ref[...], hidden, preferred_element_type=jnp.float32)
    for r in range(rows):
        grid = field_ref[r].astype(jnp.float32)
        out_ref[r] = (grid + down[:, r * lon_cells : (r + 1) * lon_cells]).astype(out_ref.dtype)


def finish(field, back, lon_table, local_weight, local_bias, gate_weight, up_weight, down_weight, block=4):
    rows, chans, lon_cells = field.shape
    modes = back.shape[2]
    hid = gate_weight.shape[1]
    whole = lambda i: (0, 0)
    return pl.pallas_call(
        finish_kernel,
        out_shape=jax.ShapeDtypeStruct(field.shape, field.dtype),
        grid=(rows // block,),
        in_specs=[
            pl.BlockSpec((block, chans, lon_cells), lambda i: (i, 0, 0)),
            pl.BlockSpec((block, chans, modes), lambda i: (i, 0, 0)),
            pl.BlockSpec((modes, lon_cells), whole),
            pl.BlockSpec((chans, chans), whole),
            pl.BlockSpec((chans, 1), whole),
            pl.BlockSpec((hid, chans), whole),
            pl.BlockSpec((hid, chans), whole),
            pl.BlockSpec((chans, hid), whole),
        ],
        out_specs=pl.BlockSpec((block, chans, lon_cells), lambda i: (i, 0, 0)),
        cost_estimate=pl.CostEstimate(
            flops=2 * rows * lon_cells * chans * (modes + chans + 3 * hid),
            transcendentals=rows * lon_cells * (chans + 2 * hid),
            bytes_accessed=4 * field.size + 2 * back.size,
        ),
    )(
        field,
        back,
        lon_table.T,
        local_weight.T,
        local_bias.reshape(chans, 1),
        gate_weight.T,
        up_weight.T,
        down_weight.T,
    )


def body(field, spectral_weight, local_weight, local_bias, gate_weight, up_weight, down_weight):
    high = lax.Precision.HIGHEST
    batch, levels, lat_rows, chans, lon_cells = field.shape
    ranks = lax.axis_size("rows")
    lat_total = lat_rows * ranks
    lat_modes = spectral_weight.shape[1]
    lon_modes = spectral_weight.shape[2] * ranks
    lon_table = cas_rows(jnp.arange(lon_cells, dtype=jnp.int32), lon_cells, lon_modes).astype(
        jnp.bfloat16
    )
    lat_table = cas_rows(jnp.arange(lat_total, dtype=jnp.int32), lat_total, lat_modes).reshape(
        ranks, lat_rows, lat_modes
    )
    per = lon_modes // ranks
    along = jnp.einsum("xm,blncx->mblnc", lon_table, field, preferred_element_type=jnp.float32)
    along = along.astype(jnp.bfloat16).reshape((ranks, per) + along.shape[1:])
    along = lax.all_to_all(along, "rows", 0, 0, tiled=True).astype(jnp.float32)
    modes = jnp.einsum("sjblnc,snk->jblkc", along, lat_table, precision=high)
    modes = modes.astype(jnp.bfloat16)
    padded = extended(modes, (("lev", 2),), 1)
    mixed = jnp.einsum(
        "kjco,jblkc->jblko",
        spectral_weight[0],
        padded[:, :, 0:levels],
        preferred_element_type=jnp.float32,
    )
    mixed = mixed + jnp.einsum(
        "kjco,jblkc->jblko",
        spectral_weight[1],
        padded[:, :, 1 : levels + 1],
        preferred_element_type=jnp.float32,
    )
    mixed = mixed + jnp.einsum(
        "kjco,jblkc->jblko",
        spectral_weight[2],
        padded[:, :, 2 : levels + 2],
        preferred_element_type=jnp.float32,
    )
    mixed_b = mixed.astype(jnp.bfloat16)
    values = jnp.einsum(
        "rnk,jblko->rjblno", lat_table, mixed_b.astype(jnp.float32), precision=high
    )
    values = lax.all_to_all(values.astype(jnp.bfloat16), "rows", 0, 0, tiled=True)
    back_b = jnp.transpose(values, (2, 3, 4, 5, 0, 1)).reshape(
        batch, levels, lat_rows, chans, lon_modes
    )

    result = finish(
        field.reshape(batch * levels * lat_rows, chans, lon_cells),
        back_b.reshape(batch * levels * lat_rows, chans, lon_modes),
        lon_table,
        local_weight,
        local_bias,
        gate_weight,
        up_weight,
        down_weight,
    )
    return result.reshape(batch, levels, lat_rows, chans, lon_cells)


def solution(mesh):
    return jax.shard_map(
        body,
        mesh=mesh,
        in_specs=(
            P(None, "lev", "rows", None, None),
            P(None, None, "rows", None, None),
            P(),
            P(),
            P(),
            P(),
            P(),
        ),
        out_specs=P(None, "lev", "rows", None, None),
        check_vma=False,
    )
```

```python
import functools
import math

import jax
import jax.numpy as jnp
from jax import lax
from jax.experimental import pallas as pl
from jax.experimental.pallas import tpu as pltpu
from jax.sharding import PartitionSpec as P


def extended(cells, sides, width):
    for axis, dim in sides:
        count = lax.axis_size(axis)
        ends = count - 1
        head = lax.slice_in_dim(cells, 0, width, axis=dim)
        tail = lax.slice_in_dim(cells, cells.shape[dim] - width, cells.shape[dim], axis=dim)
        cells = jnp.concatenate(
            [
                lax.ppermute(tail, axis, [(i, (i + 1) % count) for i in range(ends)]),
                cells,
                lax.ppermute(head, axis, [((i + 1) % count, i) for i in range(ends)]),
            ],
            axis=dim,
        )
    return cells


def cas_rows(positions, count, modes):
    freq = jnp.arange(modes, dtype=jnp.int32) - modes // 2
    turns = positions[:, None] * freq[None, :] % count
    angle = 2.0 * math.pi / count * turns.astype(jnp.float32)
    return (jnp.cos(angle) + jnp.sin(angle)) / math.sqrt(count)


def halo_kernel(axis, x_ref, below_ref, above_ref, send_sems, recv_sems):
    count = lax.axis_size(axis)
    me = lax.axis_index(axis)
    up = lax.rem(me + 1, count)
    down = lax.rem(me + count - 1, count)
    barrier = pltpu.get_barrier_semaphore()
    for neighbour in (down, up):
        pl.semaphore_signal(
            barrier, inc=1, device_id={axis: neighbour}, device_id_type=pl.DeviceIdType.MESH
        )
    pl.semaphore_wait(barrier, 2)
    copies = [
        pltpu.make_async_remote_copy(
            src_ref=x_ref,
            dst_ref=dst,
            send_sem=send_sems.at[slot],
            recv_sem=recv_sems.at[slot],
            device_id={axis: peer},
            device_id_type=pl.DeviceIdType.MESH,
        )
        for slot, (dst, peer) in enumerate(((below_ref, up), (above_ref, down)))
    ]
    for copy in copies:
        copy.start()
    for copy in copies:
        copy.wait()


def halo(x, axis):
    return pl.pallas_call(
        functools.partial(halo_kernel, axis),
        out_shape=(jax.ShapeDtypeStruct(x.shape, x.dtype),) * 2,
        in_specs=[pl.BlockSpec(memory_space=pl.ANY)],
        out_specs=(pl.BlockSpec(memory_space=pl.ANY),) * 2,
        scratch_shapes=[pltpu.SemaphoreType.DMA((2,)), pltpu.SemaphoreType.DMA((2,))],
        compiler_params=pltpu.CompilerParams(collective_id=0, has_side_effects=True),
    )(x)


def finish_kernel(field_ref, back_ref, lon_ref, local_ref, bias_ref, gate_ref, up_ref, down_ref, out_ref):
    sqrt_half = math.sqrt(0.5)
    rows, _, lon_cells = field_ref.shape
    acts = []
    for r in range(rows):
        lhs = jnp.concatenate([back_ref[r], local_ref[...]], axis=1)
        rhs = jnp.concatenate([lon_ref[...], field_ref[r]], axis=0)
        value = jnp.dot(lhs, rhs, preferred_element_type=jnp.float32) + bias_ref[...]
        acts.append((0.5 * value * (1.0 + lax.erf(value * sqrt_half))).astype(jnp.bfloat16))
    act = jnp.concatenate(acts, axis=1)
    gate = jnp.dot(gate_ref[...], act, preferred_element_type=jnp.float32)
    upper = jnp.dot(up_ref[...], act, preferred_element_type=jnp.float32)
    hidden = (0.5 * gate * (1.0 + jnp.tanh(0.5 * gate)) * upper).astype(jnp.bfloat16)
    down = jnp.dot(down_ref[...], hidden, preferred_element_type=jnp.float32)
    for r in range(rows):
        grid = field_ref[r].astype(jnp.float32)
        out_ref[r] = (grid + down[:, r * lon_cells : (r + 1) * lon_cells]).astype(out_ref.dtype)


def finish(field, back, lon_table, local_weight, local_bias, gate_weight, up_weight, down_weight, block=4):
    rows, chans, lon_cells = field.shape
    modes = back.shape[2]
    hid = gate_weight.shape[1]
    whole = lambda i: (0, 0)
    return pl.pallas_call(
        finish_kernel,
        out_shape=jax.ShapeDtypeStruct(field.shape, field.dtype),
        grid=(rows // block,),
        in_specs=[
            pl.BlockSpec((block, chans, lon_cells), lambda i: (i, 0, 0)),
            pl.BlockSpec((block, chans, modes), lambda i: (i, 0, 0)),
            pl.BlockSpec((modes, lon_cells), whole),
            pl.BlockSpec((chans, chans), whole),
            pl.BlockSpec((chans, 1), whole),
            pl.BlockSpec((hid, chans), whole),
            pl.BlockSpec((hid, chans), whole),
            pl.BlockSpec((chans, hid), whole),
        ],
        out_specs=pl.BlockSpec((block, chans, lon_cells), lambda i: (i, 0, 0)),
        cost_estimate=pl.CostEstimate(
            flops=2 * rows * lon_cells * chans * (modes + chans + 3 * hid),
            transcendentals=rows * lon_cells * (chans + 2 * hid),
            bytes_accessed=4 * field.size + 2 * back.size,
        ),
    )(
        field,
        back,
        lon_table.T,
        local_weight.T,
        local_bias.reshape(chans, 1),
        gate_weight.T,
        up_weight.T,
        down_weight.T,
    )


def body(field, spectral_weight, local_weight, local_bias, gate_weight, up_weight, down_weight):
    high = lax.Precision.HIGHEST
    batch, levels, lat_rows, chans, lon_cells = field.shape
    ranks = lax.axis_size("rows")
    lat_total = lat_rows * ranks
    lat_modes = spectral_weight.shape[1]
    lon_modes = spectral_weight.shape[2] * ranks
    lon_table = cas_rows(jnp.arange(lon_cells, dtype=jnp.int32), lon_cells, lon_modes).astype(
        jnp.bfloat16
    )
    lat_table = cas_rows(jnp.arange(lat_total, dtype=jnp.int32), lat_total, lat_modes).reshape(
        ranks, lat_rows, lat_modes
    )
    per = lon_modes // ranks
    along = jnp.einsum("xm,blncx->mblnc", lon_table, field, preferred_element_type=jnp.float32)
    along = along.astype(jnp.bfloat16).reshape((ranks, per) + along.shape[1:])
    along = lax.all_to_all(along, "rows", 0, 0, tiled=True).astype(jnp.float32)
    modes = jnp.einsum("sjblnc,snk->jblkc", along, lat_table, precision=high)
    modes = modes.astype(jnp.bfloat16)
    below, above = halo(modes, "lev")
    level = lax.axis_index("lev")
    below = jnp.where(level > 0, below, jnp.zeros_like(below))
    above = jnp.where(level < lax.axis_size("lev") - 1, above, jnp.zeros_like(above))
    stacked = jnp.stack([below, modes, above])
    mixed = jnp.einsum(
        "dkjco,djblkc->jblko", spectral_weight, stacked, preferred_element_type=jnp.float32
    )
    mixed_b = mixed.astype(jnp.bfloat16)
    values = jnp.einsum(
        "rnk,jblko->rjblno", lat_table, mixed_b.astype(jnp.float32), precision=high
    )
    values = lax.all_to_all(values.astype(jnp.bfloat16), "rows", 0, 0, tiled=True)
    back_b = jnp.transpose(values, (2, 3, 4, 5, 0, 1)).reshape(
        batch, levels, lat_rows, chans, lon_modes
    )

    result = finish(
        field.reshape(batch * levels * lat_rows, chans, lon_cells),
        back_b.reshape(batch * levels * lat_rows, chans, lon_modes),
        lon_table,
        local_weight,
        local_bias,
        gate_weight,
        up_weight,
        down_weight,
    )
    return result.reshape(batch, levels, lat_rows, chans, lon_cells)


def solution(mesh):
    return jax.shard_map(
        body,
        mesh=mesh,
        in_specs=(
            P(None, "lev", "rows", None, None),
            P(None, None, "rows", None, None),
            P(),
            P(),
            P(),
            P(),
            P(),
        ),
        out_specs=P(None, "lev", "rows", None, None),
        check_vma=False,
    )
```

```python
import math

import jax
import jax.numpy as jnp
from jax import lax
from jax.experimental import pallas as pl
from jax.experimental.pallas import tpu as pltpu
from jax.sharding import PartitionSpec as P


def extended(cells, sides, width):
    for axis, dim in sides:
        count = lax.axis_size(axis)
        ends = count - 1
        head = lax.slice_in_dim(cells, 0, width, axis=dim)
        tail = lax.slice_in_dim(cells, cells.shape[dim] - width, cells.shape[dim], axis=dim)
        cells = jnp.concatenate(
            [
                lax.ppermute(tail, axis, [(i, (i + 1) % count) for i in range(ends)]),
                cells,
                lax.ppermute(head, axis, [((i + 1) % count, i) for i in range(ends)]),
            ],
            axis=dim,
        )
    return cells


def cas_rows(positions, count, modes):
    freq = jnp.arange(modes, dtype=jnp.int32) - modes // 2
    turns = positions[:, None] * freq[None, :] % count
    angle = 2.0 * math.pi / count * turns.astype(jnp.float32)
    return (jnp.cos(angle) + jnp.sin(angle)) / math.sqrt(count)


def finish_kernel(field_ref, back_ref, lon_ref, local_ref, bias_ref, gate_ref, up_ref, down_ref, out_ref):
    sqrt_half = math.sqrt(0.5)
    rows, _, lon_cells = field_ref.shape
    acts = []
    for r in range(rows):
        lhs = jnp.concatenate([back_ref[r], local_ref[...]], axis=1)
        rhs = jnp.concatenate([lon_ref[...], field_ref[r]], axis=0)
        value = jnp.dot(lhs, rhs, preferred_element_type=jnp.float32) + bias_ref[...]
        acts.append((0.5 * value * (1.0 + lax.erf(value * sqrt_half))).astype(jnp.bfloat16))
    act = jnp.concatenate(acts, axis=1)
    half = jnp.dot(gate_ref[...], act, preferred_element_type=jnp.float32)
    upper = jnp.dot(up_ref[...], act, preferred_element_type=jnp.float32)
    hidden = ((half + half * jnp.tanh(half)) * upper).astype(jnp.bfloat16)
    down = jnp.dot(down_ref[...], hidden, preferred_element_type=jnp.float32)
    for r in range(rows):
        grid = field_ref[r].astype(jnp.float32)
        out_ref[r] = (grid + down[:, r * lon_cells : (r + 1) * lon_cells]).astype(out_ref.dtype)


def finish(field, back, lon_table, local_weight, local_bias, gate_weight, up_weight, down_weight, block=4):
    rows, chans, lon_cells = field.shape
    modes = back.shape[2]
    hid = gate_weight.shape[1]
    whole = lambda i: (0, 0)
    return pl.pallas_call(
        finish_kernel,
        out_shape=jax.ShapeDtypeStruct(field.shape, field.dtype),
        grid=(rows // block,),
        in_specs=[
            pl.BlockSpec((block, chans, lon_cells), lambda i: (i, 0, 0)),
            pl.BlockSpec((block, chans, modes), lambda i: (i, 0, 0)),
            pl.BlockSpec((modes, lon_cells), whole),
            pl.BlockSpec((chans, chans), whole),
            pl.BlockSpec((chans, 1), whole),
            pl.BlockSpec((hid, chans), whole),
            pl.BlockSpec((hid, chans), whole),
            pl.BlockSpec((chans, hid), whole),
        ],
        out_specs=pl.BlockSpec((block, chans, lon_cells), lambda i: (i, 0, 0)),
        cost_estimate=pl.CostEstimate(
            flops=2 * rows * lon_cells * chans * (modes + chans + 3 * hid),
            transcendentals=rows * lon_cells * (chans + 2 * hid),
            bytes_accessed=4 * field.size + 2 * back.size,
        ),
    )(
        field,
        back,
        lon_table.T,
        local_weight.T,
        local_bias.reshape(chans, 1),
        (gate_weight * 0.5).astype(gate_weight.dtype).T,
        up_weight.T,
        down_weight.T,
    )


def body(field, spectral_weight, local_weight, local_bias, gate_weight, up_weight, down_weight):
    high = lax.Precision.HIGHEST
    batch, levels, lat_rows, chans, lon_cells = field.shape
    ranks = lax.axis_size("rows")
    lat_total = lat_rows * ranks
    lat_modes = spectral_weight.shape[1]
    lon_modes = spectral_weight.shape[2] * ranks
    lon_table = cas_rows(jnp.arange(lon_cells, dtype=jnp.int32), lon_cells, lon_modes).astype(
        jnp.bfloat16
    )
    lat_table = cas_rows(jnp.arange(lat_total, dtype=jnp.int32), lat_total, lat_modes).reshape(
        ranks, lat_rows, lat_modes
    )
    per = lon_modes // ranks
    along = jnp.einsum("xm,blncx->mblnc", lon_table, field, preferred_element_type=jnp.float32)
    along = along.astype(jnp.bfloat16).reshape((ranks, per) + along.shape[1:])
    along = lax.all_to_all(along, "rows", 0, 0, tiled=True)
    lat_high = lat_table.astype(jnp.bfloat16)
    lat_low = (lat_table - lat_high.astype(jnp.float32)).astype(jnp.bfloat16)

    def by_lat(spec, data, first):
        pair = [(lat_high, data), (data, lat_high)][first]
        rest = [(lat_low, data), (data, lat_low)][first]
        return jnp.einsum(spec, *pair, preferred_element_type=jnp.float32) + jnp.einsum(
            spec, *rest, preferred_element_type=jnp.float32
        )

    modes = by_lat("sjblnc,snk->jblkc", along, 1)
    modes = modes.astype(jnp.bfloat16)
    padded = extended(modes, (("lev", 2),), 1)
    mixed = jnp.einsum(
        "kjco,jblkc->jblko",
        spectral_weight[0],
        padded[:, :, 0:levels],
        preferred_element_type=jnp.float32,
    )
    mixed = mixed + jnp.einsum(
        "kjco,jblkc->jblko",
        spectral_weight[1],
        padded[:, :, 1 : levels + 1],
        preferred_element_type=jnp.float32,
    )
    mixed = mixed + jnp.einsum(
        "kjco,jblkc->jblko",
        spectral_weight[2],
        padded[:, :, 2 : levels + 2],
        preferred_element_type=jnp.float32,
    )
    mixed_b = mixed.astype(jnp.bfloat16)
    values = by_lat("rnk,jblko->rjblno", mixed_b, 0)
    values = lax.all_to_all(values.astype(jnp.bfloat16), "rows", 0, 0, tiled=True)
    back_b = jnp.transpose(values, (2, 3, 4, 5, 0, 1)).reshape(
        batch, levels, lat_rows, chans, lon_modes
    )

    result = finish(
        field.reshape(batch * levels * lat_rows, chans, lon_cells),
        back_b.reshape(batch * levels * lat_rows, chans, lon_modes),
        lon_table,
        local_weight,
        local_bias,
        gate_weight,
        up_weight,
        down_weight,
    )
    return result.reshape(batch, levels, lat_rows, chans, lon_cells)


def solution(mesh):
    return jax.shard_map(
        body,
        mesh=mesh,
        in_specs=(
            P(None, "lev", "rows", None, None),
            P(None, None, "rows", None, None),
            P(),
            P(),
            P(),
            P(),
            P(),
        ),
        out_specs=P(None, "lev", "rows", None, None),
        check_vma=False,
    )
```

```python
import math

import jax
import jax.numpy as jnp
from jax import lax
from jax.experimental import pallas as pl
from jax.experimental.pallas import tpu as pltpu
from jax.sharding import PartitionSpec as P


def extended(cells, sides, width):
    for axis, dim in sides:
        count = lax.axis_size(axis)
        ends = count - 1
        head = lax.slice_in_dim(cells, 0, width, axis=dim)
        tail = lax.slice_in_dim(cells, cells.shape[dim] - width, cells.shape[dim], axis=dim)
        cells = jnp.concatenate(
            [
                lax.ppermute(tail, axis, [(i, (i + 1) % count) for i in range(ends)]),
                cells,
                lax.ppermute(head, axis, [((i + 1) % count, i) for i in range(ends)]),
            ],
            axis=dim,
        )
    return cells


def cas_rows(positions, count, modes):
    freq = jnp.arange(modes, dtype=jnp.int32) - modes // 2
    turns = positions[:, None] * freq[None, :] % count
    angle = 2.0 * math.pi / count * turns.astype(jnp.float32)
    return (jnp.cos(angle) + jnp.sin(angle)) / math.sqrt(count)


def finish_kernel(field_ref, back_ref, lon_ref, local_ref, bias_ref, gate_ref, up_ref, down_ref, out_ref):
    sqrt_half = math.sqrt(0.5)
    rows, _, lon_cells = field_ref.shape
    acts = []
    for r in range(rows):
        lhs = jnp.concatenate([back_ref[r], local_ref[...]], axis=1)
        rhs = jnp.concatenate([lon_ref[...], field_ref[r]], axis=0)
        value = jnp.dot(lhs, rhs, preferred_element_type=jnp.float32) + bias_ref[...]
        acts.append((0.5 * value * (1.0 + lax.erf(value * sqrt_half))).astype(jnp.bfloat16))
    act = jnp.concatenate(acts, axis=1)
    half = jnp.dot(gate_ref[...], act, preferred_element_type=jnp.float32)
    upper = jnp.dot(up_ref[...], act, preferred_element_type=jnp.float32)
    hidden = ((half + half * jnp.tanh(half)) * upper).astype(jnp.bfloat16)
    down = jnp.dot(down_ref[...], hidden, preferred_element_type=jnp.float32)
    for r in range(rows):
        grid = field_ref[r].astype(jnp.float32)
        out_ref[r] = (grid + down[:, r * lon_cells : (r + 1) * lon_cells]).astype(out_ref.dtype)


def finish(field, back, lon_table, local_weight, local_bias, gate_weight, up_weight, down_weight, block=4):
    rows, chans, lon_cells = field.shape
    modes = back.shape[2]
    hid = gate_weight.shape[1]
    whole = lambda i: (0, 0)
    return pl.pallas_call(
        finish_kernel,
        out_shape=jax.ShapeDtypeStruct(field.shape, field.dtype),
        grid=(rows // block,),
        in_specs=[
            pl.BlockSpec((block, chans, lon_cells), lambda i: (i, 0, 0)),
            pl.BlockSpec((block, chans, modes), lambda i: (i, 0, 0)),
            pl.BlockSpec((modes, lon_cells), whole),
            pl.BlockSpec((chans, chans), whole),
            pl.BlockSpec((chans, 1), whole),
            pl.BlockSpec((hid, chans), whole),
            pl.BlockSpec((hid, chans), whole),
            pl.BlockSpec((chans, hid), whole),
        ],
        out_specs=pl.BlockSpec((block, chans, lon_cells), lambda i: (i, 0, 0)),
        cost_estimate=pl.CostEstimate(
            flops=2 * rows * lon_cells * chans * (modes + chans + 3 * hid),
            transcendentals=rows * lon_cells * (chans + 2 * hid),
            bytes_accessed=4 * field.size + 2 * back.size,
        ),
    )(
        field,
        back,
        lon_table.T,
        local_weight.T,
        local_bias.reshape(chans, 1),
        (gate_weight * 0.5).astype(gate_weight.dtype).T,
        up_weight.T,
        down_weight.T,
    )


def body(field, spectral_weight, local_weight, local_bias, gate_weight, up_weight, down_weight):
    high = lax.Precision.HIGHEST
    batch, levels, lat_rows, chans, lon_cells = field.shape
    ranks = lax.axis_size("rows")
    lat_total = lat_rows * ranks
    lat_modes = spectral_weight.shape[1]
    lon_modes = spectral_weight.shape[2] * ranks
    lon_table = cas_rows(jnp.arange(lon_cells, dtype=jnp.int32), lon_cells, lon_modes).astype(
        jnp.bfloat16
    )
    lat_table = cas_rows(jnp.arange(lat_total, dtype=jnp.int32), lat_total, lat_modes).reshape(
        ranks, lat_rows, lat_modes
    )
    per = lon_modes // ranks
    along = jnp.einsum("xm,blncx->mblnc", lon_table, field, preferred_element_type=jnp.float32)
    along = along.astype(jnp.bfloat16).reshape((ranks, per) + along.shape[1:])
    along = lax.all_to_all(along, "rows", 0, 0, tiled=True).astype(jnp.float32)
    modes = jnp.einsum("sjblnc,snk->jblkc", along, lat_table, precision=high)
    modes = modes.astype(jnp.bfloat16)
    padded = extended(modes, (("lev", 2),), 1)
    mixed = jnp.einsum(
        "kjco,jblkc->jblko",
        spectral_weight[0],
        padded[:, :, 0:levels],
        preferred_element_type=jnp.float32,
    )
    mixed = mixed + jnp.einsum(
        "kjco,jblkc->jblko",
        spectral_weight[1],
        padded[:, :, 1 : levels + 1],
        preferred_element_type=jnp.float32,
    )
    mixed = mixed + jnp.einsum(
        "kjco,jblkc->jblko",
        spectral_weight[2],
        padded[:, :, 2 : levels + 2],
        preferred_element_type=jnp.float32,
    )
    mixed_b = mixed.astype(jnp.bfloat16)
    values = jnp.einsum(
        "rnk,jblko->rjblno", lat_table, mixed_b.astype(jnp.float32), precision=high
    )
    values = lax.all_to_all(values.astype(jnp.bfloat16), "rows", 0, 0, tiled=True)
    back_b = jnp.transpose(values, (2, 3, 4, 5, 0, 1)).reshape(
        batch, levels, lat_rows, chans, lon_modes
    )

    result = finish(
        field.reshape(batch * levels * lat_rows, chans, lon_cells),
        back_b.reshape(batch * levels * lat_rows, chans, lon_modes),
        lon_table,
        local_weight,
        local_bias,
        gate_weight,
        up_weight,
        down_weight,
    )
    return result.reshape(batch, levels, lat_rows, chans, lon_cells)


def solution(mesh):
    return jax.shard_map(
        body,
        mesh=mesh,
        in_specs=(
            P(None, "lev", "rows", None, None),
            P(None, None, "rows", None, None),
            P(),
            P(),
            P(),
            P(),
            P(),
        ),
        out_specs=P(None, "lev", "rows", None, None),
        check_vma=False,
    )
```

```python
import math

import jax
import jax.numpy as jnp
from jax import lax
from jax.experimental import pallas as pl
from jax.experimental.pallas import tpu as pltpu
from jax.sharding import PartitionSpec as P


def extended(cells, sides, width):
    for axis, dim in sides:
        count = lax.axis_size(axis)
        ends = count - 1
        head = lax.slice_in_dim(cells, 0, width, axis=dim)
        tail = lax.slice_in_dim(cells, cells.shape[dim] - width, cells.shape[dim], axis=dim)
        cells = jnp.concatenate(
            [
                lax.ppermute(tail, axis, [(i, (i + 1) % count) for i in range(ends)]),
                cells,
                lax.ppermute(head, axis, [((i + 1) % count, i) for i in range(ends)]),
            ],
            axis=dim,
        )
    return cells


def cas_rows(positions, count, modes):
    freq = jnp.arange(modes, dtype=jnp.int32) - modes // 2
    turns = positions[:, None] * freq[None, :] % count
    angle = 2.0 * math.pi / count * turns.astype(jnp.float32)
    return (jnp.cos(angle) + jnp.sin(angle)) / math.sqrt(count)


def finish_kernel(field_ref, back_ref, lon_ref, local_ref, bias_ref, gate_up_ref, down_ref, out_ref):
    sqrt_half = math.sqrt(0.5)
    rows, _, lon_cells = field_ref.shape
    acts = []
    for r in range(rows):
        lhs = jnp.concatenate([back_ref[r], local_ref[...]], axis=1)
        rhs = jnp.concatenate([lon_ref[...], field_ref[r]], axis=0)
        value = jnp.dot(lhs, rhs, preferred_element_type=jnp.float32) + bias_ref[...]
        acts.append((0.5 * value * (1.0 + lax.erf(value * sqrt_half))).astype(jnp.bfloat16))
    act = jnp.concatenate(acts, axis=1)
    both = jnp.dot(gate_up_ref[...], act, preferred_element_type=jnp.float32)
    hid = gate_up_ref.shape[0] // 2
    half, upper = both[:hid], both[hid:]
    hidden = ((half + half * jnp.tanh(half)) * upper).astype(jnp.bfloat16)
    down = jnp.dot(down_ref[...], hidden, preferred_element_type=jnp.float32)
    for r in range(rows):
        grid = field_ref[r].astype(jnp.float32)
        out_ref[r] = (grid + down[:, r * lon_cells : (r + 1) * lon_cells]).astype(out_ref.dtype)


def finish(field, back, lon_table, local_weight, local_bias, gate_weight, up_weight, down_weight, block=8):
    rows, chans, lon_cells = field.shape
    modes = back.shape[2]
    hid = gate_weight.shape[1]
    whole = lambda i: (0, 0)
    return pl.pallas_call(
        finish_kernel,
        out_shape=jax.ShapeDtypeStruct(field.shape, field.dtype),
        grid=(rows // block,),
        in_specs=[
            pl.BlockSpec((block, chans, lon_cells), lambda i: (i, 0, 0)),
            pl.BlockSpec((block, chans, modes), lambda i: (i, 0, 0)),
            pl.BlockSpec((modes, lon_cells), whole),
            pl.BlockSpec((chans, chans), whole),
            pl.BlockSpec((chans, 1), whole),
            pl.BlockSpec((2 * hid, chans), whole),
            pl.BlockSpec((chans, hid), whole),
        ],
        out_specs=pl.BlockSpec((block, chans, lon_cells), lambda i: (i, 0, 0)),
        cost_estimate=pl.CostEstimate(
            flops=2 * rows * lon_cells * chans * (modes + chans + 3 * hid),
            transcendentals=rows * lon_cells * (chans + 2 * hid),
            bytes_accessed=4 * field.size + 2 * back.size,
        ),
    )(
        field,
        back,
        lon_table.T,
        local_weight.T,
        local_bias.reshape(chans, 1),
        jnp.concatenate([(gate_weight * 0.5).astype(gate_weight.dtype), up_weight], axis=1).T,
        down_weight.T,
    )


def body(field, spectral_weight, local_weight, local_bias, gate_weight, up_weight, down_weight):
    high = lax.Precision.HIGHEST
    batch, levels, lat_rows, chans, lon_cells = field.shape
    ranks = lax.axis_size("rows")
    lat_total = lat_rows * ranks
    lat_modes = spectral_weight.shape[1]
    lon_modes = spectral_weight.shape[2] * ranks
    lon_table = cas_rows(jnp.arange(lon_cells, dtype=jnp.int32), lon_cells, lon_modes).astype(
        jnp.bfloat16
    )
    lat_table = cas_rows(jnp.arange(lat_total, dtype=jnp.int32), lat_total, lat_modes).reshape(
        ranks, lat_rows, lat_modes
    )
    per = lon_modes // ranks
    along = jnp.einsum("xm,blncx->mblnc", lon_table, field, preferred_element_type=jnp.float32)
    along = along.astype(jnp.bfloat16).reshape((ranks, per) + along.shape[1:])
    along = lax.all_to_all(along, "rows", 0, 0, tiled=True).astype(jnp.float32)
    modes = jnp.einsum("sjblnc,snk->jblkc", along, lat_table, precision=high)
    modes = modes.astype(jnp.bfloat16)
    padded = extended(modes, (("lev", 2),), 1)
    mixed = jnp.einsum(
        "kjco,jblkc->jblko",
        spectral_weight[0],
        padded[:, :, 0:levels],
        preferred_element_type=jnp.float32,
    )
    mixed = mixed + jnp.einsum(
        "kjco,jblkc->jblko",
        spectral_weight[1],
        padded[:, :, 1 : levels + 1],
        preferred_element_type=jnp.float32,
    )
    mixed = mixed + jnp.einsum(
        "kjco,jblkc->jblko",
        spectral_weight[2],
        padded[:, :, 2 : levels + 2],
        preferred_element_type=jnp.float32,
    )
    mixed_b = mixed.astype(jnp.bfloat16)
    values = jnp.einsum(
        "rnk,jblko->rjblno", lat_table, mixed_b.astype(jnp.float32), precision=high
    )
    values = lax.all_to_all(values.astype(jnp.bfloat16), "rows", 0, 0, tiled=True)
    back_b = jnp.transpose(values, (2, 3, 4, 5, 0, 1)).reshape(
        batch, levels, lat_rows, chans, lon_modes
    )

    result = finish(
        field.reshape(batch * levels * lat_rows, chans, lon_cells),
        back_b.reshape(batch * levels * lat_rows, chans, lon_modes),
        lon_table,
        local_weight,
        local_bias,
        gate_weight,
        up_weight,
        down_weight,
    )
    return result.reshape(batch, levels, lat_rows, chans, lon_cells)


def solution(mesh):
    return jax.shard_map(
        body,
        mesh=mesh,
        in_specs=(
            P(None, "lev", "rows", None, None),
            P(None, None, "rows", None, None),
            P(),
            P(),
            P(),
            P(),
            P(),
        ),
        out_specs=P(None, "lev", "rows", None, None),
        check_vma=False,
    )
```

```python
import math

import jax
import jax.numpy as jnp
from jax import lax
from jax.experimental import pallas as pl
from jax.experimental.pallas import tpu as pltpu
from jax.sharding import PartitionSpec as P


def extended(cells, sides, width):
    for axis, dim in sides:
        count = lax.axis_size(axis)
        ends = count - 1
        head = lax.slice_in_dim(cells, 0, width, axis=dim)
        tail = lax.slice_in_dim(cells, cells.shape[dim] - width, cells.shape[dim], axis=dim)
        cells = jnp.concatenate(
            [
                lax.ppermute(tail, axis, [(i, (i + 1) % count) for i in range(ends)]),
                cells,
                lax.ppermute(head, axis, [((i + 1) % count, i) for i in range(ends)]),
            ],
            axis=dim,
        )
    return cells


def cas_rows(positions, count, modes):
    freq = jnp.arange(modes, dtype=jnp.int32) - modes // 2
    turns = positions[:, None] * freq[None, :] % count
    angle = 2.0 * math.pi / count * turns.astype(jnp.float32)
    return (jnp.cos(angle) + jnp.sin(angle)) / math.sqrt(count)


def finish_kernel(field_ref, back_ref, lon_ref, local_ref, bias_ref, gate_up_ref, down_ref, out_ref):
    sqrt_half = math.sqrt(0.5)
    rows, _, lon_cells = field_ref.shape
    acts = []
    for r in range(rows):
        lhs = jnp.concatenate([back_ref[r], local_ref[...]], axis=1)
        rhs = jnp.concatenate([lon_ref[...], field_ref[r]], axis=0)
        value = jnp.dot(lhs, rhs, preferred_element_type=jnp.float32) + bias_ref[...]
        acts.append((0.5 * value * (1.0 + lax.erf(value * sqrt_half))).astype(jnp.bfloat16))
    act = jnp.concatenate(acts, axis=1)
    both = jnp.dot(gate_up_ref[...], act, preferred_element_type=jnp.float32)
    hid = gate_up_ref.shape[0] // 2
    half, upper = both[:hid], both[hid:]
    hidden = ((half + half * jnp.tanh(half)) * upper).astype(jnp.bfloat16)
    down = jnp.dot(down_ref[...], hidden, preferred_element_type=jnp.float32)
    for r in range(rows):
        grid = field_ref[r].astype(jnp.float32)
        out_ref[r] = (grid + down[:, r * lon_cells : (r + 1) * lon_cells]).astype(out_ref.dtype)


def finish(field, back, lon_table, local_weight, local_bias, gate_weight, up_weight, down_weight, block=8):
    rows, chans, lon_cells = field.shape
    modes = back.shape[2]
    hid = gate_weight.shape[1]
    whole = lambda i: (0, 0)
    return pl.pallas_call(
        finish_kernel,
        out_shape=jax.ShapeDtypeStruct(field.shape, field.dtype),
        grid=(rows // block,),
        in_specs=[
            pl.BlockSpec((block, chans, lon_cells), lambda i: (i, 0, 0)),
            pl.BlockSpec((block, chans, modes), lambda i: (i, 0, 0)),
            pl.BlockSpec((modes, lon_cells), whole),
            pl.BlockSpec((chans, chans), whole),
            pl.BlockSpec((chans, 1), whole),
            pl.BlockSpec((2 * hid, chans), whole),
            pl.BlockSpec((chans, hid), whole),
        ],
        out_specs=pl.BlockSpec((block, chans, lon_cells), lambda i: (i, 0, 0)),
        cost_estimate=pl.CostEstimate(
            flops=2 * rows * lon_cells * chans * (modes + chans + 3 * hid),
            transcendentals=rows * lon_cells * (chans + 2 * hid),
            bytes_accessed=4 * field.size + 2 * back.size,
        ),
    )(
        field,
        back,
        lon_table.T,
        local_weight.T,
        local_bias.reshape(chans, 1),
        jnp.concatenate([(gate_weight * 0.5).astype(gate_weight.dtype), up_weight], axis=1).T,
        down_weight.T,
    )


def body(field, spectral_weight, local_weight, local_bias, gate_weight, up_weight, down_weight):
    high = lax.Precision.HIGHEST
    batch, levels, lat_rows, chans, lon_cells = field.shape
    ranks = lax.axis_size("rows")
    lat_total = lat_rows * ranks
    lat_modes = spectral_weight.shape[1]
    lon_modes = spectral_weight.shape[2] * ranks
    lon_table = cas_rows(jnp.arange(lon_cells, dtype=jnp.int32), lon_cells, lon_modes).astype(
        jnp.bfloat16
    )
    lat_table = cas_rows(jnp.arange(lat_total, dtype=jnp.int32), lat_total, lat_modes).reshape(
        ranks, lat_rows, lat_modes
    )
    per = lon_modes // ranks
    along = jnp.einsum("xm,blncx->mblnc", lon_table, field, preferred_element_type=jnp.float32)
    along = along.astype(jnp.bfloat16).reshape((ranks, per) + along.shape[1:])
    along = lax.all_to_all(along, "rows", 0, 0, tiled=True).astype(jnp.float32)
    modes = jnp.einsum("sjblnc,snk->jblkc", along, lat_table, precision=high)
    modes = modes.astype(jnp.bfloat16)
    padded = extended(modes, (("lev", 2),), 1)
    stacked = jnp.stack([padded[:, :, shift : shift + levels] for shift in range(3)])
    mixed = jnp.einsum(
        "dkjco,djblkc->jblko", spectral_weight, stacked, preferred_element_type=jnp.float32
    )
    mixed_b = mixed.astype(jnp.bfloat16)
    values = jnp.einsum(
        "rnk,jblko->rjblno", lat_table, mixed_b.astype(jnp.float32), precision=high
    )
    values = lax.all_to_all(values.astype(jnp.bfloat16), "rows", 0, 0, tiled=True)
    back_b = jnp.transpose(values, (2, 3, 4, 5, 0, 1)).reshape(
        batch, levels, lat_rows, chans, lon_modes
    )

    result = finish(
        field.reshape(batch * levels * lat_rows, chans, lon_cells),
        back_b.reshape(batch * levels * lat_rows, chans, lon_modes),
        lon_table,
        local_weight,
        local_bias,
        gate_weight,
        up_weight,
        down_weight,
    )
    return result.reshape(batch, levels, lat_rows, chans, lon_cells)


def solution(mesh):
    return jax.shard_map(
        body,
        mesh=mesh,
        in_specs=(
            P(None, "lev", "rows", None, None),
            P(None, None, "rows", None, None),
            P(),
            P(),
            P(),
            P(),
            P(),
        ),
        out_specs=P(None, "lev", "rows", None, None),
        check_vma=False,
    )
```

```python
import math

import jax
import jax.numpy as jnp
from jax import lax
from jax.experimental import pallas as pl
from jax.experimental.pallas import tpu as pltpu
from jax.sharding import PartitionSpec as P


def extended(cells, sides, width):
    for axis, dim in sides:
        count = lax.axis_size(axis)
        ends = count - 1
        head = lax.slice_in_dim(cells, 0, width, axis=dim)
        tail = lax.slice_in_dim(cells, cells.shape[dim] - width, cells.shape[dim], axis=dim)
        cells = jnp.concatenate(
            [
                lax.ppermute(tail, axis, [(i, (i + 1) % count) for i in range(ends)]),
                cells,
                lax.ppermute(head, axis, [((i + 1) % count, i) for i in range(ends)]),
            ],
            axis=dim,
        )
    return cells


def cas_rows(positions, count, modes):
    freq = jnp.arange(modes, dtype=jnp.int32) - modes // 2
    turns = positions[:, None] * freq[None, :] % count
    angle = 2.0 * math.pi / count * turns.astype(jnp.float32)
    return (jnp.cos(angle) + jnp.sin(angle)) / math.sqrt(count)


def along_kernel(lon_ref, field_ref, out_ref):
    rows, chans, lon_cells = field_ref.shape
    grid = field_ref[...].reshape(rows * chans, lon_cells)
    out_ref[...] = lax.dot_general(
        lon_ref[...], grid, (((1,), (1,)), ((), ())), preferred_element_type=jnp.float32
    ).astype(out_ref.dtype)


def along_modes(field, lon_table, block=8):
    rows, chans, lon_cells = field.shape
    modes = lon_table.shape[1]
    return pl.pallas_call(
        along_kernel,
        out_shape=jax.ShapeDtypeStruct((modes, rows * chans), jnp.bfloat16),
        grid=(rows // block,),
        in_specs=[
            pl.BlockSpec((modes, lon_cells), lambda i: (0, 0)),
            pl.BlockSpec((block, chans, lon_cells), lambda i: (i, 0, 0)),
        ],
        out_specs=pl.BlockSpec((modes, block * chans), lambda i: (0, i)),
        cost_estimate=pl.CostEstimate(
            flops=2 * modes * rows * chans * lon_cells,
            transcendentals=0,
            bytes_accessed=2 * field.size + 2 * modes * rows * chans,
        ),
    )(lon_table.T, field)


def finish_kernel(field_ref, back_ref, lon_ref, local_ref, bias_ref, gate_up_ref, down_ref, out_ref):
    sqrt_half = math.sqrt(0.5)
    rows, _, lon_cells = field_ref.shape
    acts = []
    for r in range(rows):
        lhs = jnp.concatenate([back_ref[r], local_ref[...]], axis=1)
        rhs = jnp.concatenate([lon_ref[...], field_ref[r]], axis=0)
        value = jnp.dot(lhs, rhs, preferred_element_type=jnp.float32) + bias_ref[...]
        acts.append((0.5 * value * (1.0 + lax.erf(value * sqrt_half))).astype(jnp.bfloat16))
    act = jnp.concatenate(acts, axis=1)
    both = jnp.dot(gate_up_ref[...], act, preferred_element_type=jnp.float32)
    hid = gate_up_ref.shape[0] // 2
    half, upper = both[:hid], both[hid:]
    hidden = ((half + half * jnp.tanh(half)) * upper).astype(jnp.bfloat16)
    down = jnp.dot(down_ref[...], hidden, preferred_element_type=jnp.float32)
    for r in range(rows):
        grid = field_ref[r].astype(jnp.float32)
        out_ref[r] = (grid + down[:, r * lon_cells : (r + 1) * lon_cells]).astype(out_ref.dtype)


def finish(field, back, lon_table, local_weight, local_bias, gate_weight, up_weight, down_weight, block=8):
    rows, chans, lon_cells = field.shape
    modes = back.shape[2]
    hid = gate_weight.shape[1]
    whole = lambda i: (0, 0)
    return pl.pallas_call(
        finish_kernel,
        out_shape=jax.ShapeDtypeStruct(field.shape, field.dtype),
        grid=(rows // block,),
        in_specs=[
            pl.BlockSpec((block, chans, lon_cells), lambda i: (i, 0, 0)),
            pl.BlockSpec((block, chans, modes), lambda i: (i, 0, 0)),
            pl.BlockSpec((modes, lon_cells), whole),
            pl.BlockSpec((chans, chans), whole),
            pl.BlockSpec((chans, 1), whole),
            pl.BlockSpec((2 * hid, chans), whole),
            pl.BlockSpec((chans, hid), whole),
        ],
        out_specs=pl.BlockSpec((block, chans, lon_cells), lambda i: (i, 0, 0)),
        cost_estimate=pl.CostEstimate(
            flops=2 * rows * lon_cells * chans * (modes + chans + 3 * hid),
            transcendentals=rows * lon_cells * (chans + 2 * hid),
            bytes_accessed=4 * field.size + 2 * back.size,
        ),
    )(
        field,
        back,
        lon_table.T,
        local_weight.T,
        local_bias.reshape(chans, 1),
        jnp.concatenate([(gate_weight * 0.5).astype(gate_weight.dtype), up_weight], axis=1).T,
        down_weight.T,
    )


def body(field, spectral_weight, local_weight, local_bias, gate_weight, up_weight, down_weight):
    high = lax.Precision.HIGHEST
    batch, levels, lat_rows, chans, lon_cells = field.shape
    ranks = lax.axis_size("rows")
    lat_total = lat_rows * ranks
    lat_modes = spectral_weight.shape[1]
    lon_modes = spectral_weight.shape[2] * ranks
    lon_table = cas_rows(jnp.arange(lon_cells, dtype=jnp.int32), lon_cells, lon_modes).astype(
        jnp.bfloat16
    )
    lat_table = cas_rows(jnp.arange(lat_total, dtype=jnp.int32), lat_total, lat_modes).reshape(
        ranks, lat_rows, lat_modes
    )
    per = lon_modes // ranks
    along = along_modes(field.reshape(-1, chans, lon_cells), lon_table)
    along = along.reshape((ranks, per, batch, levels, lat_rows, chans))
    along = lax.all_to_all(along, "rows", 0, 0, tiled=True).astype(jnp.float32)
    modes = jnp.einsum("sjblnc,snk->jblkc", along, lat_table, precision=high)
    modes = modes.astype(jnp.bfloat16)
    padded = extended(modes, (("lev", 2),), 1)
    mixed = jnp.einsum(
        "kjco,jblkc->jblko",
        spectral_weight[0],
        padded[:, :, 0:levels],
        preferred_element_type=jnp.float32,
    )
    mixed = mixed + jnp.einsum(
        "kjco,jblkc->jblko",
        spectral_weight[1],
        padded[:, :, 1 : levels + 1],
        preferred_element_type=jnp.float32,
    )
    mixed = mixed + jnp.einsum(
        "kjco,jblkc->jblko",
        spectral_weight[2],
        padded[:, :, 2 : levels + 2],
        preferred_element_type=jnp.float32,
    )
    mixed_b = mixed.astype(jnp.bfloat16)
    values = jnp.einsum(
        "rnk,jblko->rjblno", lat_table, mixed_b.astype(jnp.float32), precision=high
    )
    values = lax.all_to_all(values.astype(jnp.bfloat16), "rows", 0, 0, tiled=True)
    back_b = jnp.transpose(values, (2, 3, 4, 5, 0, 1)).reshape(
        batch, levels, lat_rows, chans, lon_modes
    )

    result = finish(
        field.reshape(batch * levels * lat_rows, chans, lon_cells),
        back_b.reshape(batch * levels * lat_rows, chans, lon_modes),
        lon_table,
        local_weight,
        local_bias,
        gate_weight,
        up_weight,
        down_weight,
    )
    return result.reshape(batch, levels, lat_rows, chans, lon_cells)


def solution(mesh):
    return jax.shard_map(
        body,
        mesh=mesh,
        in_specs=(
            P(None, "lev", "rows", None, None),
            P(None, None, "rows", None, None),
            P(),
            P(),
            P(),
            P(),
            P(),
        ),
        out_specs=P(None, "lev", "rows", None, None),
        check_vma=False,
    )
```

```python
import math

import jax
import jax.numpy as jnp
from jax import lax
from jax.experimental import pallas as pl
from jax.experimental.pallas import tpu as pltpu
from jax.sharding import PartitionSpec as P


def extended(cells, sides, width):
    for axis, dim in sides:
        count = lax.axis_size(axis)
        ends = count - 1
        head = lax.slice_in_dim(cells, 0, width, axis=dim)
        tail = lax.slice_in_dim(cells, cells.shape[dim] - width, cells.shape[dim], axis=dim)
        cells = jnp.concatenate(
            [
                lax.ppermute(tail, axis, [(i, (i + 1) % count) for i in range(ends)]),
                cells,
                lax.ppermute(head, axis, [((i + 1) % count, i) for i in range(ends)]),
            ],
            axis=dim,
        )
    return cells


def cas_rows(positions, count, modes):
    freq = jnp.arange(modes, dtype=jnp.int32) - modes // 2
    turns = positions[:, None] * freq[None, :] % count
    angle = 2.0 * math.pi / count * turns.astype(jnp.float32)
    return (jnp.cos(angle) + jnp.sin(angle)) / math.sqrt(count)


def finish_kernel(field_ref, back_ref, lon_ref, local_ref, bias_ref, gate_up_ref, down_ref, out_ref):
    sqrt_half = math.sqrt(0.5)
    rows, _, lon_cells = field_ref.shape
    acts = []
    for r in range(rows):
        lhs = jnp.concatenate([back_ref[:, r, :], local_ref[...].T], axis=0)
        rhs = jnp.concatenate([lon_ref[...], field_ref[r]], axis=0)
        value = lax.dot_general(
            lhs, rhs, (((0,), (0,)), ((), ())), preferred_element_type=jnp.float32
        ) + bias_ref[...]
        acts.append((0.5 * value * (1.0 + lax.erf(value * sqrt_half))).astype(jnp.bfloat16))
    act = jnp.concatenate(acts, axis=1)
    both = jnp.dot(gate_up_ref[...], act, preferred_element_type=jnp.float32)
    hid = gate_up_ref.shape[0] // 2
    half, upper = both[:hid], both[hid:]
    hidden = ((half + half * jnp.tanh(half)) * upper).astype(jnp.bfloat16)
    down = jnp.dot(down_ref[...], hidden, preferred_element_type=jnp.float32)
    for r in range(rows):
        grid = field_ref[r].astype(jnp.float32)
        out_ref[r] = (grid + down[:, r * lon_cells : (r + 1) * lon_cells]).astype(out_ref.dtype)


def finish(field, back, lon_table, local_weight, local_bias, gate_weight, up_weight, down_weight, block=8):
    rows, chans, lon_cells = field.shape
    modes = back.shape[0]
    hid = gate_weight.shape[1]
    whole = lambda i: (0, 0)
    return pl.pallas_call(
        finish_kernel,
        out_shape=jax.ShapeDtypeStruct(field.shape, field.dtype),
        grid=(rows // block,),
        in_specs=[
            pl.BlockSpec((block, chans, lon_cells), lambda i: (i, 0, 0)),
            pl.BlockSpec((modes, block, chans), lambda i: (0, i, 0)),
            pl.BlockSpec((modes, lon_cells), whole),
            pl.BlockSpec((chans, chans), whole),
            pl.BlockSpec((chans, 1), whole),
            pl.BlockSpec((2 * hid, chans), whole),
            pl.BlockSpec((chans, hid), whole),
        ],
        out_specs=pl.BlockSpec((block, chans, lon_cells), lambda i: (i, 0, 0)),
        cost_estimate=pl.CostEstimate(
            flops=2 * rows * lon_cells * chans * (modes + chans + 3 * hid),
            transcendentals=rows * lon_cells * (chans + 2 * hid),
            bytes_accessed=4 * field.size + 2 * back.size,
        ),
    )(
        field,
        back,
        lon_table.T,
        local_weight.T,
        local_bias.reshape(chans, 1),
        jnp.concatenate([(gate_weight * 0.5).astype(gate_weight.dtype), up_weight], axis=1).T,
        down_weight.T,
    )


def body(field, spectral_weight, local_weight, local_bias, gate_weight, up_weight, down_weight):
    high = lax.Precision.HIGHEST
    batch, levels, lat_rows, chans, lon_cells = field.shape
    ranks = lax.axis_size("rows")
    lat_total = lat_rows * ranks
    lat_modes = spectral_weight.shape[1]
    lon_modes = spectral_weight.shape[2] * ranks
    lon_table = cas_rows(jnp.arange(lon_cells, dtype=jnp.int32), lon_cells, lon_modes).astype(
        jnp.bfloat16
    )
    lat_table = cas_rows(jnp.arange(lat_total, dtype=jnp.int32), lat_total, lat_modes).reshape(
        ranks, lat_rows, lat_modes
    )
    per = lon_modes // ranks
    along = jnp.einsum("xm,blncx->mblnc", lon_table, field, preferred_element_type=jnp.float32)
    along = along.astype(jnp.bfloat16).reshape((ranks, per) + along.shape[1:])
    along = lax.all_to_all(along, "rows", 0, 0, tiled=True).astype(jnp.float32)
    modes = jnp.einsum("sjblnc,snk->jblkc", along, lat_table, precision=high)
    modes = modes.astype(jnp.bfloat16)
    padded = extended(modes, (("lev", 2),), 1)
    mixed = jnp.einsum(
        "kjco,jblkc->jblko",
        spectral_weight[0],
        padded[:, :, 0:levels],
        preferred_element_type=jnp.float32,
    )
    mixed = mixed + jnp.einsum(
        "kjco,jblkc->jblko",
        spectral_weight[1],
        padded[:, :, 1 : levels + 1],
        preferred_element_type=jnp.float32,
    )
    mixed = mixed + jnp.einsum(
        "kjco,jblkc->jblko",
        spectral_weight[2],
        padded[:, :, 2 : levels + 2],
        preferred_element_type=jnp.float32,
    )
    mixed_b = mixed.astype(jnp.bfloat16)
    values = jnp.einsum(
        "rnk,jblko->rjblno", lat_table, mixed_b.astype(jnp.float32), precision=high
    )
    values = lax.all_to_all(values.astype(jnp.bfloat16), "rows", 0, 0, tiled=True)
    back_b = values.reshape(lon_modes, batch * levels * lat_rows, chans)

    result = finish(
        field.reshape(batch * levels * lat_rows, chans, lon_cells),
        back_b,
        lon_table,
        local_weight,
        local_bias,
        gate_weight,
        up_weight,
        down_weight,
    )
    return result.reshape(batch, levels, lat_rows, chans, lon_cells)


def solution(mesh):
    return jax.shard_map(
        body,
        mesh=mesh,
        in_specs=(
            P(None, "lev", "rows", None, None),
            P(None, None, "rows", None, None),
            P(),
            P(),
            P(),
            P(),
            P(),
        ),
        out_specs=P(None, "lev", "rows", None, None),
        check_vma=False,
    )
```

```python
import math

import jax
import jax.numpy as jnp
from jax import lax
from jax.experimental import pallas as pl
from jax.experimental.pallas import tpu as pltpu
from jax.sharding import PartitionSpec as P


def extended(cells, sides, width):
    for axis, dim in sides:
        count = lax.axis_size(axis)
        ends = count - 1
        head = lax.slice_in_dim(cells, 0, width, axis=dim)
        tail = lax.slice_in_dim(cells, cells.shape[dim] - width, cells.shape[dim], axis=dim)
        cells = jnp.concatenate(
            [
                lax.ppermute(tail, axis, [(i, (i + 1) % count) for i in range(ends)]),
                cells,
                lax.ppermute(head, axis, [((i + 1) % count, i) for i in range(ends)]),
            ],
            axis=dim,
        )
    return cells


def cas_rows(positions, count, modes):
    freq = jnp.arange(modes, dtype=jnp.int32) - modes // 2
    turns = positions[:, None] * freq[None, :] % count
    angle = 2.0 * math.pi / count * turns.astype(jnp.float32)
    return (jnp.cos(angle) + jnp.sin(angle)) / math.sqrt(count)


def finish_kernel(field_ref, back_ref, lon_ref, local_ref, bias_ref, gate_up_ref, down_ref, out_ref):
    sqrt_half = math.sqrt(0.5)
    rows, _, lon_cells = field_ref.shape
    acts = []
    for r in range(rows):
        lhs = jnp.concatenate([back_ref[r], local_ref[...]], axis=1)
        rhs = jnp.concatenate([lon_ref[...], field_ref[r]], axis=0)
        value = jnp.dot(lhs, rhs, preferred_element_type=jnp.float32) + bias_ref[...]
        acts.append((0.5 * value * (1.0 + lax.erf(value * sqrt_half))).astype(jnp.bfloat16))
    act = jnp.concatenate(acts, axis=1)
    both = jnp.dot(gate_up_ref[...], act, preferred_element_type=jnp.float32)
    hid = gate_up_ref.shape[0] // 2
    half, upper = both[:hid], both[hid:]
    hidden = ((half + half * jnp.tanh(half)) * upper).astype(jnp.bfloat16)
    down = jnp.dot(down_ref[...], hidden, preferred_element_type=jnp.float32)
    for r in range(rows):
        grid = field_ref[r].astype(jnp.float32)
        out_ref[r] = (grid + down[:, r * lon_cells : (r + 1) * lon_cells]).astype(out_ref.dtype)


def finish(field, back, lon_table, local_weight, local_bias, gate_weight, up_weight, down_weight, block=8):
    rows, chans, lon_cells = field.shape
    modes = back.shape[2]
    hid = gate_weight.shape[1]
    whole = lambda i: (0, 0)
    return pl.pallas_call(
        finish_kernel,
        out_shape=jax.ShapeDtypeStruct(field.shape, field.dtype),
        grid=(rows // block,),
        in_specs=[
            pl.BlockSpec((block, chans, lon_cells), lambda i: (i, 0, 0)),
            pl.BlockSpec((block, chans, modes), lambda i: (i, 0, 0)),
            pl.BlockSpec((modes, lon_cells), whole),
            pl.BlockSpec((chans, chans), whole),
            pl.BlockSpec((chans, 1), whole),
            pl.BlockSpec((2 * hid, chans), whole),
            pl.BlockSpec((chans, hid), whole),
        ],
        out_specs=pl.BlockSpec((block, chans, lon_cells), lambda i: (i, 0, 0)),
        cost_estimate=pl.CostEstimate(
            flops=2 * rows * lon_cells * chans * (modes + chans + 3 * hid),
            transcendentals=rows * lon_cells * (chans + 2 * hid),
            bytes_accessed=4 * field.size + 2 * back.size,
        ),
    )(
        field,
        back,
        lon_table.T,
        local_weight.T,
        local_bias.reshape(chans, 1),
        jnp.concatenate([(gate_weight * 0.5).astype(gate_weight.dtype), up_weight], axis=1).T,
        down_weight.T,
    )


def body(field, spectral_weight, local_weight, local_bias, gate_weight, up_weight, down_weight):
    batch, levels, lat_rows, chans, lon_cells = field.shape
    ranks = lax.axis_size("rows")
    lat_total = lat_rows * ranks
    lat_modes = spectral_weight.shape[1]
    lon_modes = spectral_weight.shape[2] * ranks
    lon_table = cas_rows(jnp.arange(lon_cells, dtype=jnp.int32), lon_cells, lon_modes).astype(
        jnp.bfloat16
    )
    lat_table = cas_rows(jnp.arange(lat_total, dtype=jnp.int32), lat_total, lat_modes).reshape(
        ranks, lat_rows, lat_modes
    )
    per = lon_modes // ranks
    along = jnp.einsum("xm,blncx->mblnc", lon_table, field, preferred_element_type=jnp.float32)
    along = along.astype(jnp.bfloat16).reshape((ranks, per) + along.shape[1:])
    along = lax.all_to_all(along, "rows", 0, 0, tiled=True)
    lat_b = lat_table.astype(jnp.bfloat16)
    modes = jnp.einsum("sjblnc,snk->jblkc", along, lat_b, preferred_element_type=jnp.float32)
    modes = modes.astype(jnp.bfloat16)
    padded = extended(modes, (("lev", 2),), 1)
    mixed = jnp.einsum(
        "kjco,jblkc->jblko",
        spectral_weight[0],
        padded[:, :, 0:levels],
        preferred_element_type=jnp.float32,
    )
    mixed = mixed + jnp.einsum(
        "kjco,jblkc->jblko",
        spectral_weight[1],
        padded[:, :, 1 : levels + 1],
        preferred_element_type=jnp.float32,
    )
    mixed = mixed + jnp.einsum(
        "kjco,jblkc->jblko",
        spectral_weight[2],
        padded[:, :, 2 : levels + 2],
        preferred_element_type=jnp.float32,
    )
    mixed_b = mixed.astype(jnp.bfloat16)
    values = jnp.einsum("rnk,jblko->rjblno", lat_b, mixed_b, preferred_element_type=jnp.float32)
    values = lax.all_to_all(values.astype(jnp.bfloat16), "rows", 0, 0, tiled=True)
    back_b = jnp.transpose(values, (2, 3, 4, 5, 0, 1)).reshape(
        batch, levels, lat_rows, chans, lon_modes
    )

    result = finish(
        field.reshape(batch * levels * lat_rows, chans, lon_cells),
        back_b.reshape(batch * levels * lat_rows, chans, lon_modes),
        lon_table,
        local_weight,
        local_bias,
        gate_weight,
        up_weight,
        down_weight,
    )
    return result.reshape(batch, levels, lat_rows, chans, lon_cells)


def solution(mesh):
    return jax.shard_map(
        body,
        mesh=mesh,
        in_specs=(
            P(None, "lev", "rows", None, None),
            P(None, None, "rows", None, None),
            P(),
            P(),
            P(),
            P(),
            P(),
        ),
        out_specs=P(None, "lev", "rows", None, None),
        check_vma=False,
    )
```

```python
import math

import jax
import jax.numpy as jnp
from jax import lax
from jax.experimental import pallas as pl
from jax.experimental.pallas import tpu as pltpu
from jax.sharding import PartitionSpec as P


def extended(cells, sides, width):
    for axis, dim in sides:
        count = lax.axis_size(axis)
        ends = count - 1
        head = lax.slice_in_dim(cells, 0, width, axis=dim)
        tail = lax.slice_in_dim(cells, cells.shape[dim] - width, cells.shape[dim], axis=dim)
        cells = jnp.concatenate(
            [
                lax.ppermute(tail, axis, [(i, (i + 1) % count) for i in range(ends)]),
                cells,
                lax.ppermute(head, axis, [((i + 1) % count, i) for i in range(ends)]),
            ],
            axis=dim,
        )
    return cells


def cas_rows(positions, count, modes):
    freq = jnp.arange(modes, dtype=jnp.int32) - modes // 2
    turns = positions[:, None] * freq[None, :] % count
    angle = 2.0 * math.pi / count * turns.astype(jnp.float32)
    return (jnp.cos(angle) + jnp.sin(angle)) / math.sqrt(count)


def finish_kernel(field_ref, back_ref, lon_ref, local_ref, bias_ref, gate_up_ref, down_ref, out_ref):
    sqrt_half = math.sqrt(0.5)
    rows, _, lon_cells = field_ref.shape
    acts = []
    for r in range(rows):
        lhs = jnp.concatenate([back_ref[:, r, :], local_ref[...].T], axis=0)
        rhs = jnp.concatenate([lon_ref[...], field_ref[r]], axis=0)
        value = lax.dot_general(
            lhs, rhs, (((0,), (0,)), ((), ())), preferred_element_type=jnp.float32
        ) + bias_ref[...]
        acts.append((0.5 * value * (1.0 + lax.erf(value * sqrt_half))).astype(jnp.bfloat16))
    act = jnp.concatenate(acts, axis=1)
    both = jnp.dot(gate_up_ref[...], act, preferred_element_type=jnp.float32)
    hid = gate_up_ref.shape[0] // 2
    half, upper = both[:hid], both[hid:]
    hidden = ((half + half * jnp.tanh(half)) * upper).astype(jnp.bfloat16)
    down = jnp.dot(down_ref[...], hidden, preferred_element_type=jnp.float32)
    for r in range(rows):
        grid = field_ref[r].astype(jnp.float32)
        out_ref[r] = (grid + down[:, r * lon_cells : (r + 1) * lon_cells]).astype(out_ref.dtype)


def finish(field, back, lon_table, local_weight, local_bias, gate_weight, up_weight, down_weight, block=8):
    rows, chans, lon_cells = field.shape
    modes = back.shape[0]
    hid = gate_weight.shape[1]
    whole = lambda i: (0, 0)
    return pl.pallas_call(
        finish_kernel,
        out_shape=jax.ShapeDtypeStruct(field.shape, field.dtype),
        grid=(rows // block,),
        in_specs=[
            pl.BlockSpec((block, chans, lon_cells), lambda i: (i, 0, 0)),
            pl.BlockSpec((modes, block, chans), lambda i: (0, i, 0)),
            pl.BlockSpec((modes, lon_cells), whole),
            pl.BlockSpec((chans, chans), whole),
            pl.BlockSpec((chans, 1), whole),
            pl.BlockSpec((2 * hid, chans), whole),
            pl.BlockSpec((chans, hid), whole),
        ],
        out_specs=pl.BlockSpec((block, chans, lon_cells), lambda i: (i, 0, 0)),
        cost_estimate=pl.CostEstimate(
            flops=2 * rows * lon_cells * chans * (modes + chans + 3 * hid),
            transcendentals=rows * lon_cells * (chans + 2 * hid),
            bytes_accessed=4 * field.size + 2 * back.size,
        ),
    )(
        field,
        back,
        lon_table.T,
        local_weight.T,
        local_bias.reshape(chans, 1),
        jnp.concatenate([(gate_weight * 0.5).astype(gate_weight.dtype), up_weight], axis=1).T,
        down_weight.T,
    )


def body(field, spectral_weight, local_weight, local_bias, gate_weight, up_weight, down_weight):
    batch, levels, lat_rows, chans, lon_cells = field.shape
    ranks = lax.axis_size("rows")
    lat_total = lat_rows * ranks
    lat_modes = spectral_weight.shape[1]
    lon_modes = spectral_weight.shape[2] * ranks
    lon_table = cas_rows(jnp.arange(lon_cells, dtype=jnp.int32), lon_cells, lon_modes).astype(
        jnp.bfloat16
    )
    lat_table = cas_rows(jnp.arange(lat_total, dtype=jnp.int32), lat_total, lat_modes).reshape(
        ranks, lat_rows, lat_modes
    )
    per = lon_modes // ranks
    along = jnp.einsum("xm,blncx->mblnc", lon_table, field, preferred_element_type=jnp.float32)
    along = along.astype(jnp.bfloat16).reshape((ranks, per) + along.shape[1:])
    along = lax.all_to_all(along, "rows", 0, 0, tiled=True)
    lat_b = lat_table.astype(jnp.bfloat16)
    modes = jnp.einsum("sjblnc,snk->jblkc", along, lat_b, preferred_element_type=jnp.float32)
    modes = modes.astype(jnp.bfloat16)
    padded = extended(modes, (("lev", 2),), 1)
    mixed = jnp.einsum(
        "kjco,jblkc->jblko",
        spectral_weight[0],
        padded[:, :, 0:levels],
        preferred_element_type=jnp.float32,
    )
    mixed = mixed + jnp.einsum(
        "kjco,jblkc->jblko",
        spectral_weight[1],
        padded[:, :, 1 : levels + 1],
        preferred_element_type=jnp.float32,
    )
    mixed = mixed + jnp.einsum(
        "kjco,jblkc->jblko",
        spectral_weight[2],
        padded[:, :, 2 : levels + 2],
        preferred_element_type=jnp.float32,
    )
    mixed_b = mixed.astype(jnp.bfloat16)
    values = jnp.einsum("rnk,jblko->rjblno", lat_b, mixed_b, preferred_element_type=jnp.float32)
    values = lax.all_to_all(values.astype(jnp.bfloat16), "rows", 0, 0, tiled=True)
    back_b = values.reshape(lon_modes, batch * levels * lat_rows, chans)

    result = finish(
        field.reshape(batch * levels * lat_rows, chans, lon_cells),
        back_b,
        lon_table,
        local_weight,
        local_bias,
        gate_weight,
        up_weight,
        down_weight,
    )
    return result.reshape(batch, levels, lat_rows, chans, lon_cells)


def solution(mesh):
    return jax.shard_map(
        body,
        mesh=mesh,
        in_specs=(
            P(None, "lev", "rows", None, None),
            P(None, None, "rows", None, None),
            P(),
            P(),
            P(),
            P(),
            P(),
        ),
        out_specs=P(None, "lev", "rows", None, None),
        check_vma=False,
    )
```

```python
import math

import jax
import jax.numpy as jnp
from jax import lax
from jax.experimental import pallas as pl
from jax.experimental.pallas import tpu as pltpu
from jax.sharding import PartitionSpec as P


def extended(cells, sides, width):
    for axis, dim in sides:
        count = lax.axis_size(axis)
        ends = count - 1
        head = lax.slice_in_dim(cells, 0, width, axis=dim)
        tail = lax.slice_in_dim(cells, cells.shape[dim] - width, cells.shape[dim], axis=dim)
        cells = jnp.concatenate(
            [
                lax.ppermute(tail, axis, [(i, (i + 1) % count) for i in range(ends)]),
                cells,
                lax.ppermute(head, axis, [((i + 1) % count, i) for i in range(ends)]),
            ],
            axis=dim,
        )
    return cells


def cas_rows(positions, count, modes):
    freq = jnp.arange(modes, dtype=jnp.int32) - modes // 2
    turns = positions[:, None] * freq[None, :] % count
    angle = 2.0 * math.pi / count * turns.astype(jnp.float32)
    return (jnp.cos(angle) + jnp.sin(angle)) / math.sqrt(count)


def finish_kernel(field_ref, back_ref, lon_ref, local_ref, bias_ref, gate_up_ref, down_ref, out_ref):
    sqrt_half = math.sqrt(0.5)
    rows, _, lon_cells = field_ref.shape
    acts = []
    for r in range(rows):
        lhs = jnp.concatenate([back_ref[:, r, :], local_ref[...].T], axis=0)
        rhs = jnp.concatenate([lon_ref[...], field_ref[r]], axis=0)
        value = lax.dot_general(
            lhs, rhs, (((0,), (0,)), ((), ())), preferred_element_type=jnp.float32
        ) + bias_ref[...]
        acts.append((0.5 * value * (1.0 + lax.erf(value * sqrt_half))).astype(jnp.bfloat16))
    act = jnp.concatenate(acts, axis=1)
    both = jnp.dot(gate_up_ref[...], act, preferred_element_type=jnp.float32)
    hid = gate_up_ref.shape[0] // 2
    half, upper = both[:hid], both[hid:]
    half = half.astype(jnp.bfloat16)
    hidden = (half + half * jnp.tanh(half)) * upper.astype(jnp.bfloat16)
    down = jnp.dot(down_ref[...], hidden, preferred_element_type=jnp.float32)
    for r in range(rows):
        grid = field_ref[r].astype(jnp.float32)
        out_ref[r] = (grid + down[:, r * lon_cells : (r + 1) * lon_cells]).astype(out_ref.dtype)


def finish(field, back, lon_table, local_weight, local_bias, gate_weight, up_weight, down_weight, block=8):
    rows, chans, lon_cells = field.shape
    modes = back.shape[0]
    hid = gate_weight.shape[1]
    whole = lambda i: (0, 0)
    return pl.pallas_call(
        finish_kernel,
        out_shape=jax.ShapeDtypeStruct(field.shape, field.dtype),
        grid=(rows // block,),
        in_specs=[
            pl.BlockSpec((block, chans, lon_cells), lambda i: (i, 0, 0)),
            pl.BlockSpec((modes, block, chans), lambda i: (0, i, 0)),
            pl.BlockSpec((modes, lon_cells), whole),
            pl.BlockSpec((chans, chans), whole),
            pl.BlockSpec((chans, 1), whole),
            pl.BlockSpec((2 * hid, chans), whole),
            pl.BlockSpec((chans, hid), whole),
        ],
        out_specs=pl.BlockSpec((block, chans, lon_cells), lambda i: (i, 0, 0)),
        cost_estimate=pl.CostEstimate(
            flops=2 * rows * lon_cells * chans * (modes + chans + 3 * hid),
            transcendentals=rows * lon_cells * (chans + 2 * hid),
            bytes_accessed=4 * field.size + 2 * back.size,
        ),
    )(
        field,
        back,
        lon_table.T,
        local_weight.T,
        local_bias.reshape(chans, 1),
        jnp.concatenate([(gate_weight * 0.5).astype(gate_weight.dtype), up_weight], axis=1).T,
        down_weight.T,
    )


def body(field, spectral_weight, local_weight, local_bias, gate_weight, up_weight, down_weight):
    batch, levels, lat_rows, chans, lon_cells = field.shape
    ranks = lax.axis_size("rows")
    lat_total = lat_rows * ranks
    lat_modes = spectral_weight.shape[1]
    lon_modes = spectral_weight.shape[2] * ranks
    lon_table = cas_rows(jnp.arange(lon_cells, dtype=jnp.int32), lon_cells, lon_modes).astype(
        jnp.bfloat16
    )
    lat_table = cas_rows(jnp.arange(lat_total, dtype=jnp.int32), lat_total, lat_modes).reshape(
        ranks, lat_rows, lat_modes
    )
    per = lon_modes // ranks
    along = jnp.einsum("xm,blncx->mblnc", lon_table, field, preferred_element_type=jnp.float32)
    along = along.astype(jnp.bfloat16).reshape((ranks, per) + along.shape[1:])
    along = lax.all_to_all(along, "rows", 0, 0, tiled=True)
    lat_b = lat_table.astype(jnp.bfloat16)
    modes = jnp.einsum("sjblnc,snk->jblkc", along, lat_b, preferred_element_type=jnp.float32)
    modes = modes.astype(jnp.bfloat16)
    padded = extended(modes, (("lev", 2),), 1)
    mixed = jnp.einsum(
        "kjco,jblkc->jblko",
        spectral_weight[0],
        padded[:, :, 0:levels],
        preferred_element_type=jnp.float32,
    )
    mixed = mixed + jnp.einsum(
        "kjco,jblkc->jblko",
        spectral_weight[1],
        padded[:, :, 1 : levels + 1],
        preferred_element_type=jnp.float32,
    )
    mixed = mixed + jnp.einsum(
        "kjco,jblkc->jblko",
        spectral_weight[2],
        padded[:, :, 2 : levels + 2],
        preferred_element_type=jnp.float32,
    )
    mixed_b = mixed.astype(jnp.bfloat16)
    values = jnp.einsum("rnk,jblko->rjblno", lat_b, mixed_b, preferred_element_type=jnp.float32)
    values = lax.all_to_all(values.astype(jnp.bfloat16), "rows", 0, 0, tiled=True)
    back_b = values.reshape(lon_modes, batch * levels * lat_rows, chans)

    result = finish(
        field.reshape(batch * levels * lat_rows, chans, lon_cells),
        back_b,
        lon_table,
        local_weight,
        local_bias,
        gate_weight,
        up_weight,
        down_weight,
    )
    return result.reshape(batch, levels, lat_rows, chans, lon_cells)


def solution(mesh):
    return jax.shard_map(
        body,
        mesh=mesh,
        in_specs=(
            P(None, "lev", "rows", None, None),
            P(None, None, "rows", None, None),
            P(),
            P(),
            P(),
            P(),
            P(),
        ),
        out_specs=P(None, "lev", "rows", None, None),
        check_vma=False,
    )
```

```python
import math

import jax
import jax.numpy as jnp
from jax import lax
from jax.experimental import pallas as pl
from jax.experimental.pallas import tpu as pltpu
from jax.sharding import PartitionSpec as P


def extended(cells, sides, width):
    for axis, dim in sides:
        count = lax.axis_size(axis)
        ends = count - 1
        head = lax.slice_in_dim(cells, 0, width, axis=dim)
        tail = lax.slice_in_dim(cells, cells.shape[dim] - width, cells.shape[dim], axis=dim)
        cells = jnp.concatenate(
            [
                lax.ppermute(tail, axis, [(i, (i + 1) % count) for i in range(ends)]),
                cells,
                lax.ppermute(head, axis, [((i + 1) % count, i) for i in range(ends)]),
            ],
            axis=dim,
        )
    return cells


def cas_rows(positions, count, modes):
    freq = jnp.arange(modes, dtype=jnp.int32) - modes // 2
    turns = positions[:, None] * freq[None, :] % count
    angle = 2.0 * math.pi / count * turns.astype(jnp.float32)
    return (jnp.cos(angle) + jnp.sin(angle)) / math.sqrt(count)


def finish_kernel(field_ref, back_ref, lon_ref, local_ref, bias_ref, gate_up_ref, down_ref, out_ref):
    sqrt_half = math.sqrt(0.5)
    rows, _, lon_cells = field_ref.shape
    acts = []
    for r in range(rows):
        lhs = jnp.concatenate([back_ref[:, r, :], local_ref[...]], axis=0)
        rhs = jnp.concatenate([lon_ref[...], field_ref[r]], axis=0)
        value = lax.dot_general(
            lhs, rhs, (((0,), (0,)), ((), ())), preferred_element_type=jnp.float32
        ) + bias_ref[...]
        acts.append((0.5 * value * (1.0 + lax.erf(value * sqrt_half))).astype(jnp.bfloat16))
    act = jnp.concatenate(acts, axis=1)
    both = jnp.dot(gate_up_ref[...], act, preferred_element_type=jnp.float32)
    hid = gate_up_ref.shape[0] // 2
    half, upper = both[:hid], both[hid:]
    hidden = ((half + half * jnp.tanh(half)) * upper).astype(jnp.bfloat16)
    down = jnp.dot(down_ref[...], hidden, preferred_element_type=jnp.float32)
    for r in range(rows):
        grid = field_ref[r].astype(jnp.float32)
        out_ref[r] = (grid + down[:, r * lon_cells : (r + 1) * lon_cells]).astype(out_ref.dtype)


def finish(field, back, lon_table, local_weight, local_bias, gate_weight, up_weight, down_weight, block=8):
    rows, chans, lon_cells = field.shape
    modes = back.shape[0]
    hid = gate_weight.shape[1]
    whole = lambda i: (0, 0)
    return pl.pallas_call(
        finish_kernel,
        out_shape=jax.ShapeDtypeStruct(field.shape, field.dtype),
        grid=(rows // block,),
        in_specs=[
            pl.BlockSpec((block, chans, lon_cells), lambda i: (i, 0, 0)),
            pl.BlockSpec((modes, block, chans), lambda i: (0, i, 0)),
            pl.BlockSpec((modes, lon_cells), whole),
            pl.BlockSpec((chans, chans), whole),
            pl.BlockSpec((chans, 1), whole),
            pl.BlockSpec((2 * hid, chans), whole),
            pl.BlockSpec((chans, hid), whole),
        ],
        out_specs=pl.BlockSpec((block, chans, lon_cells), lambda i: (i, 0, 0)),
        cost_estimate=pl.CostEstimate(
            flops=2 * rows * lon_cells * chans * (modes + chans + 3 * hid),
            transcendentals=rows * lon_cells * (chans + 2 * hid),
            bytes_accessed=4 * field.size + 2 * back.size,
        ),
    )(
        field,
        back,
        lon_table.T,
        local_weight,
        local_bias.reshape(chans, 1),
        jnp.concatenate([(gate_weight * 0.5).astype(gate_weight.dtype), up_weight], axis=1).T,
        down_weight.T,
    )


def body(field, spectral_weight, local_weight, local_bias, gate_weight, up_weight, down_weight):
    batch, levels, lat_rows, chans, lon_cells = field.shape
    ranks = lax.axis_size("rows")
    lat_total = lat_rows * ranks
    lat_modes = spectral_weight.shape[1]
    lon_modes = spectral_weight.shape[2] * ranks
    lon_table = cas_rows(jnp.arange(lon_cells, dtype=jnp.int32), lon_cells, lon_modes).astype(
        jnp.bfloat16
    )
    lat_table = cas_rows(jnp.arange(lat_total, dtype=jnp.int32), lat_total, lat_modes).reshape(
        ranks, lat_rows, lat_modes
    )
    per = lon_modes // ranks
    along = jnp.einsum("xm,blncx->mblnc", lon_table, field, preferred_element_type=jnp.float32)
    along = along.astype(jnp.bfloat16).reshape((ranks, per) + along.shape[1:])
    along = lax.all_to_all(along, "rows", 0, 0, tiled=True)
    lat_b = lat_table.astype(jnp.bfloat16)
    modes = jnp.einsum("sjblnc,snk->jblkc", along, lat_b, preferred_element_type=jnp.float32)
    modes = modes.astype(jnp.bfloat16)
    padded = extended(modes, (("lev", 2),), 1)
    mixed = jnp.einsum(
        "kjco,jblkc->jblko",
        spectral_weight[0],
        padded[:, :, 0:levels],
        preferred_element_type=jnp.float32,
    )
    mixed = mixed + jnp.einsum(
        "kjco,jblkc->jblko",
        spectral_weight[1],
        padded[:, :, 1 : levels + 1],
        preferred_element_type=jnp.float32,
    )
    mixed = mixed + jnp.einsum(
        "kjco,jblkc->jblko",
        spectral_weight[2],
        padded[:, :, 2 : levels + 2],
        preferred_element_type=jnp.float32,
    )
    mixed_b = mixed.astype(jnp.bfloat16)
    values = jnp.einsum("rnk,jblko->rjblno", lat_b, mixed_b, preferred_element_type=jnp.float32)
    values = lax.all_to_all(values.astype(jnp.bfloat16), "rows", 0, 0, tiled=True)
    back_b = values.reshape(lon_modes, batch * levels * lat_rows, chans)

    result = finish(
        field.reshape(batch * levels * lat_rows, chans, lon_cells),
        back_b,
        lon_table,
        local_weight,
        local_bias,
        gate_weight,
        up_weight,
        down_weight,
    )
    return result.reshape(batch, levels, lat_rows, chans, lon_cells)


def solution(mesh):
    return jax.shard_map(
        body,
        mesh=mesh,
        in_specs=(
            P(None, "lev", "rows", None, None),
            P(None, None, "rows", None, None),
            P(),
            P(),
            P(),
            P(),
            P(),
        ),
        out_specs=P(None, "lev", "rows", None, None),
        check_vma=False,
    )
```
